32 devices in a mesh: pole: 2 (over y), row: 4 (over x, core), col: 4 (over z).
Axes of the slice: x: 2, y: 2, z: 4, core: 2. Of those that a mesh axis runs over, the one named last changes fastest.
Arguments:
- inverse_blocks: float32 [4096, 2048], P(('pole', 'row'), 'col'), parts along dimension 0, may hold values from -6 to 6
- lower_panel: float32 [4096, 512], P(('pole', 'row'), 'col'), parts along dimension 0, may hold values from -0.125 to 0.125
- struct_mask: int32 [16, 4], P('row', 'col'), may hold values 0 or 1
- diag_inverse: float32 [1024, 128], P(('pole', 'col')), parts along dimension 0, may hold values from -6 to 6
Outputs:
- g_panel: float32 [4096, 512], P(('pole', 'row'), 'col'), parts along dimension 0
- g_diag: float32 [1024, 128], P(('pole', 'col')), parts along dimension 0
The draws below stay inside these ranges and needn't reach their ends.
There are 2 independent parts, one for each index of `pole`. The reference program is written for one: setup_inputs(seed, part) draws one part's arguments, and reference() takes and returns one part's arrays. A program takes and returns all parts, laid end to end along the dimension named above; an argument that names none is the same for every part. Nothing has to cross between parts.
All inputs are finite; a program needn't handle non-finite values. No bound on the sum of `struct_mask` on one device may be relied on, other than what follows from the above.
Results may differ from the reference program's by a relative error of at most 0.000071.
Values sent between devices are 32-bit elements; how exact they have to be, the bound alone decides.
No kernel may reach another device: no remote copies, remote signals or barrier semaphores. Data moves between devices by JAX's collectives and lax.ppermute only.
A program may use at most 64 MiB of HBM per device.

```python
import jax
import jax.numpy as jnp
from jax import lax

B = 128
NB = 16
NK = 4


def touch_ends(drawn, stream_key, least, largest):
    longest = drawn.shape.index(max(drawn.shape))
    spots = []
    for shift in (0, 1):
        where = [jax.random.randint(jax.random.fold_in(stream_key, axis), (), 0, length) for axis, length in enumerate(drawn.shape)]
        where[longest] = (where[longest] + shift) % drawn.shape[longest]
        spots.append(tuple(where))
    return drawn.at[spots[0]].set(least).at[spots[1]].set(largest)


def shard_levels(rng, extent, pieces, smallest, largest):
    loudness = 1.0
    for dim, shards_of in pieces:
        draws = jax.random.uniform(jax.random.fold_in(jax.random.fold_in(rng, 6), dim), (shards_of,), jnp.float32, smallest / len(pieces), largest / len(pieces))
        loudness = loudness * jnp.repeat(jnp.exp(draws), extent[dim] // shards_of).reshape((-1,) + (1,) * (len(extent) - 1 - dim))
    return loudness


def noise(stream_key, dims, scale, most, shards=(), held_as=jnp.bfloat16):
    array = scale * jax.random.normal(stream_key, dims, jnp.float32)
    if shards:
        array = array * shard_levels(stream_key, dims, shards, -0.22, 0.18)
    return jnp.clip(array, -most, most).astype(held_as)


def setup_inputs(seed: int = 0, part: int = 0) -> dict:
    seeds = jax.random.split(jax.random.key(seed), 5)
    part_keys = jax.random.split(jax.random.fold_in(seeds[4], part), 5)
    inverse_blocks = noise(part_keys[0], (NB * B, NB * B), 1.0, 6.0, ((0, 4), (1, 4)), jnp.float32)
    lower_panel = noise(part_keys[1], (NB * B, NK * B), (NB * B) ** -0.5, 0.125, ((0, 4), (1, 4)), jnp.float32)
    struct_mask = touch_ends((jax.random.randint(seeds[2], (NB, NK), 0, 2) < 1).astype(jnp.int32), jax.random.fold_in(seeds[2], 1), 0, 1)
    diag_inverse = noise(part_keys[3], (NK * B, B), 1.0, 6.0, ((0, 4),), jnp.float32)
    return dict(inverse_blocks=inverse_blocks, lower_panel=lower_panel, struct_mask=struct_mask, diag_inverse=diag_inverse)


def reference(inverse_blocks, lower_panel, struct_mask, diag_inverse):
    expanded = jnp.repeat(jnp.repeat(struct_mask, B, axis=0), B, axis=1).astype(jnp.float32)
    masked = lower_panel * expanded
    product = jnp.dot(inverse_blocks, masked, precision=lax.Precision.HIGHEST, preferred_element_type=jnp.float32)
    g_panel = -product * expanded
    masked_three = masked.reshape(NB * B, NK, B)
    panel_three = g_panel.reshape(NB * B, NK, B)
    quad = jnp.einsum("jka,jkb->kab", masked_three, panel_three, precision=lax.Precision.HIGHEST)
    g_diag = diag_inverse - quad.reshape(NK * B, B)
    return g_panel, g_diag
```

```python
import functools

import jax
import jax.numpy as jnp
from jax import lax
from jax.experimental import pallas as pl
from jax.experimental.pallas import tpu as pltpu
from jax.sharding import PartitionSpec as P

GRID = ("row", "col")
VMEM = pl.BlockSpec(memory_space=pltpu.VMEM)
SMEM = pl.BlockSpec(memory_space=pltpu.SMEM)
LIMIT = pltpu.CompilerParams(vmem_limit_bytes=40 * 1024 * 1024)


def split(x):
    high = x.astype(jnp.bfloat16)
    return high, (x - high.astype(jnp.float32)).astype(jnp.bfloat16)


def dot(a, b, dims):
    return lax.dot_general(a, b, (dims, ((), ())), preferred_element_type=jnp.float32)


def masking(mask_ref, panel_ref, out_ref):
    blocks, supers = mask_ref.shape
    tall, wide = panel_ref.shape[0] // blocks, panel_ref.shape[1] // supers
    for b in range(blocks):
        for s in range(supers):
            at = (slice(b * tall, (b + 1) * tall), slice(s * wide, (s + 1) * wide))
            out_ref[at] = panel_ref[at] * mask_ref[b, s].astype(jnp.float32)


def products(count, shift_ref, a_ref, *refs):
    panels, outs = refs[:count], refs[count:]
    ah, al = split(a_ref[...])
    shift = shift_ref[0]
    for i in range(count):
        m = panels[0][...]
        for j in range(1, count):
            m = jnp.where(shift == (i ^ j), panels[j][...], m)
        mh, ml = split(m)
        both = jnp.concatenate([mh, ml], axis=1)
        width = m.shape[1]
        first = dot(ah, both, ((1,), (0,)))
        outs[i][...] = first[:, :width] + (first[:, width:] + dot(al, mh, ((1,), (0,))))


def finish(count, width, mask_ref, masked_ref, *refs):
    parts, g_ref, quad_ref = refs[:count], refs[count], refs[count + 1]
    total = parts[0][...]
    for part in parts[1:]:
        total = total + part[...]
    blocks, supers = mask_ref.shape
    tall = total.shape[0] // blocks
    for b in range(blocks):
        for s in range(supers):
            at = (slice(b * tall, (b + 1) * tall), slice(s * width, (s + 1) * width))
            g_ref[at] = total[at] * -mask_ref[b, s].astype(jnp.float32)
    for s in range(supers):
        cols = slice(s * width, (s + 1) * width)
        mh, ml = split(masked_ref[:, cols])
        gh, gl = split(g_ref[:, cols])
        rows = ((0,), (0,))
        quad_ref[cols, :] = -(dot(mh, gh, rows) + (dot(mh, gl, rows) + dot(ml, gh, rows)))


def on_device(side, inverse_blocks, lower_panel, struct_mask, diag_inverse):
    width = diag_inverse.shape[1]
    rows, cols = lower_panel.shape
    f32 = jnp.float32
    row, col = lax.axis_index("row"), lax.axis_index("col")

    def swap(x, axis, bit):
        return lax.ppermute(x, axis, [(i, i ^ bit) for i in range(side)])

    masked = pl.pallas_call(
        masking,
        out_shape=jax.ShapeDtypeStruct((rows, cols), f32),
        in_specs=[SMEM, VMEM],
        out_specs=VMEM,
        name="masking",
    )(struct_mask, lower_panel)

    turned = lax.ppermute(
        masked, GRID, [(r * side + c, c * side + r) for r in range(side) for c in range(side)]
    )
    panels = {0: turned}
    bit = side // 2
    while bit:
        for j, x in list(panels.items()):
            panels[j ^ bit] = swap(x, "row", bit)
        bit //= 2

    shift = jnp.bitwise_xor(row, col).astype(jnp.int32).reshape(1)
    partials = pl.pallas_call(
        functools.partial(products, side),
        out_shape=[jax.ShapeDtypeStruct((rows, cols), f32)] * side,
        in_specs=[SMEM] + [VMEM] * (1 + side),
        out_specs=[VMEM] * side,
        compiler_params=LIMIT,
        name="products",
    )(shift, inverse_blocks, *[panels[j] for j in range(side)])

    arrived = [partials[0]] + [swap(partials[i], "col", i) for i in range(1, side)]

    g_panel, quad = pl.pallas_call(
        functools.partial(finish, side, width),
        out_shape=[
            jax.ShapeDtypeStruct((rows, cols), f32),
            jax.ShapeDtypeStruct((cols, width), f32),
        ],
        in_specs=[SMEM] + [VMEM] * (1 + side),
        out_specs=[VMEM, VMEM],
        compiler_params=LIMIT,
        name="finish",
    )(struct_mask, masked, *arrived)

    bit = 1
    while bit < side:
        quad = quad + swap(quad, "row", bit)
        bit *= 2
    return g_panel, diag_inverse + quad


def solution(mesh):
    side = mesh.shape["row"]
    assert side == mesh.shape["col"] and side & (side - 1) == 0
    placed = (
        P(("pole", "row"), "col"),
        P(("pole", "row"), "col"),
        P("row", "col"),
        P(("pole", "col"), None),
    )
    return jax.shard_map(
        functools.partial(on_device, side),
        mesh=mesh,
        in_specs=placed,
        out_specs=(P(("pole", "row"), "col"), P(("pole", "col"), None)),
        check_vma=False,
    )
```

```python
import functools

import jax
import jax.numpy as jnp
from jax import lax
from jax.experimental import pallas as pl
from jax.experimental.pallas import tpu as pltpu
from jax.sharding import PartitionSpec as P

GRID = ("row", "col")
VMEM = pl.BlockSpec(memory_space=pltpu.VMEM)
SMEM = pl.BlockSpec(memory_space=pltpu.SMEM)
LIMIT = pltpu.CompilerParams(vmem_limit_bytes=40 * 1024 * 1024)


def split(x):
    high = x.astype(jnp.bfloat16)
    return high, (x - high.astype(jnp.float32)).astype(jnp.bfloat16)


def dot(a, b, dims):
    return lax.dot_general(a, b, (dims, ((), ())), preferred_element_type=jnp.float32)


def masking(mask_ref, panel_ref, out_ref):
    supers, blocks = mask_ref.shape
    tall, wide = panel_ref.shape[0] // blocks, panel_ref.shape[1] // supers
    for b in range(blocks):
        for s in range(supers):
            at = (slice(b * tall, (b + 1) * tall), slice(s * wide, (s + 1) * wide))
            out_ref[at] = panel_ref[at] * mask_ref[s, b].astype(jnp.float32)


def splitting(a_ref, high_ref, low_ref):
    high_ref[...], low_ref[...] = split(a_ref[...])


def products(count, shift_ref, high_ref, low_ref, *refs):
    panels, outs = refs[:count], refs[count:]
    ah, al = high_ref[...], low_ref[...]
    shift = shift_ref[0]
    for i in range(count):
        m = panels[0][...]
        for j in range(1, count):
            m = jnp.where(shift == (i ^ j), panels[j][...], m)
        mh, ml = split(m)
        both = jnp.concatenate([mh, ml], axis=1)
        width = m.shape[1]
        first = dot(ah, both, ((1,), (0,)))
        outs[i][...] = first[:, :width] + (first[:, width:] + dot(al, mh, ((1,), (0,))))


def finish(count, width, mask_ref, masked_ref, *refs):
    parts, g_ref, quad_ref = refs[:count], refs[count], refs[count + 1]
    total = parts[0][...]
    for part in parts[1:]:
        total = total + part[...]
    supers, blocks = mask_ref.shape
    tall = total.shape[0] // blocks
    for b in range(blocks):
        for s in range(supers):
            at = (slice(b * tall, (b + 1) * tall), slice(s * width, (s + 1) * width))
            g_ref[at] = total[at] * -mask_ref[s, b].astype(jnp.float32)
    for s in range(supers):
        cols = slice(s * width, (s + 1) * width)
        mh, ml = split(masked_ref[:, cols])
        gh, gl = split(g_ref[:, cols])
        rows = ((0,), (0,))
        quad_ref[cols, :] = -(dot(mh, gh, rows) + (dot(mh, gl, rows) + dot(ml, gh, rows)))


def on_device(side, inverse_blocks, lower_panel, struct_mask, diag_inverse):
    width = diag_inverse.shape[1]
    rows, cols = lower_panel.shape
    f32 = jnp.float32
    row, col = lax.axis_index("row"), lax.axis_index("col")

    def swap(x, axis, bit):
        return lax.ppermute(x, axis, [(i, i ^ bit) for i in range(side)])

    mask = struct_mask.T
    masked = pl.pallas_call(
        masking,
        out_shape=jax.ShapeDtypeStruct((rows, cols), f32),
        in_specs=[SMEM, VMEM],
        out_specs=VMEM,
        name="masking",
    )(mask, lower_panel)
    halves = pl.pallas_call(
        splitting,
        out_shape=[jax.ShapeDtypeStruct(inverse_blocks.shape, jnp.bfloat16)] * 2,
        in_specs=[VMEM],
        out_specs=[VMEM, VMEM],
        name="splitting",
    )(inverse_blocks)

    turned = lax.ppermute(
        masked, GRID, [(r * side + c, c * side + r) for r in range(side) for c in range(side)]
    )
    turned, *halves = lax.optimization_barrier((turned, *halves))
    panels = {0: turned}
    bit = side // 2
    while bit:
        for j, x in list(panels.items()):
            panels[j ^ bit] = swap(x, "row", bit)
        bit //= 2

    shift = jnp.bitwise_xor(row, col).astype(jnp.int32).reshape(1)
    partials = pl.pallas_call(
        functools.partial(products, side),
        out_shape=[jax.ShapeDtypeStruct((rows, cols), f32)] * side,
        in_specs=[SMEM] + [VMEM] * (2 + side),
        out_specs=[VMEM] * side,
        compiler_params=LIMIT,
        name="products",
    )(shift, *halves, *[panels[j] for j in range(side)])

    if side == 4:
        relayed = lax.ppermute(partials[3], "col", [(0, 1), (3, 2)])
        inner = lax.ppermute(partials[3], "col", [(1, 2), (2, 1)])
        near = swap(partials[1], "col", 1)
        far = swap(partials[2] + relayed, "col", 2)
        arrived = [partials[0], near, inner, far]
    else:
        arrived = [partials[0]] + [swap(partials[i], "col", i) for i in range(1, side)]

    g_panel, quad = pl.pallas_call(
        functools.partial(finish, len(arrived), width),
        out_shape=[
            jax.ShapeDtypeStruct((rows, cols), f32),
            jax.ShapeDtypeStruct((cols, width), f32),
        ],
        in_specs=[SMEM] + [VMEM] * (1 + len(arrived)),
        out_specs=[VMEM, VMEM],
        compiler_params=LIMIT,
        name="finish",
    )(mask, masked, *arrived)

    bit = 1
    while bit < side:
        quad = quad + swap(quad, "row", bit)
        bit *= 2
    return g_panel, diag_inverse + quad


def solution(mesh):
    side = mesh.shape["row"]
    assert side == mesh.shape["col"] and side & (side - 1) == 0
    placed = (
        P(("pole", "row"), "col"),
        P(("pole", "row"), "col"),
        P("row", "col"),
        P(("pole", "col"), None),
    )
    return jax.shard_map(
        functools.partial(on_device, side),
        mesh=mesh,
        in_specs=placed,
        out_specs=(P(("pole", "row"), "col"), P(("pole", "col"), None)),
        check_vma=False,
    )
```

```python
import functools

import jax
import jax.numpy as jnp
from jax import lax
from jax.experimental import pallas as pl
from jax.experimental.pallas import tpu as pltpu
from jax.sharding import PartitionSpec as P

GRID = ("row", "col")
VMEM = pl.BlockSpec(memory_space=pltpu.VMEM)
SMEM = pl.BlockSpec(memory_space=pltpu.SMEM)
F32 = jnp.float32
ROWS = ((0,), (0,))
INNER = ((1,), (0,))


def split(x):
    high = x.astype(jnp.bfloat16)
    return high, (x - high.astype(F32)).astype(jnp.bfloat16)


def dot(a, b, dims):
    return lax.dot_general(a, b, (dims, ((), ())), preferred_element_type=F32)


def call(body, ins, outs, args, grant, name, flops=None):
    return pl.pallas_call(
        body,
        out_shape=[jax.ShapeDtypeStruct(shape, dtype) for shape, dtype in outs],
        in_specs=ins,
        out_specs=[VMEM] * len(outs),
        compiler_params=pltpu.CompilerParams(vmem_limit_bytes=grant << 20),
        cost_estimate=flops
        and pl.CostEstimate(flops=flops, bytes_accessed=0, transcendentals=0),
        name=name,
    )(*args)


def masking(spans, mask_ref, panel_ref, *out_refs):
    supers, blocks = mask_ref.shape
    tall, wide = panel_ref.shape[0] // blocks, panel_ref.shape[1] // supers
    for (first, last), ref in zip(spans, out_refs):
        for b in range(first, last):
            for s in range(supers):
                cols = slice(s * wide, (s + 1) * wide)
                block = panel_ref[b * tall : (b + 1) * tall, cols]
                at = (b - first) * tall
                ref[at : at + tall, cols] = block * mask_ref[s, b].astype(F32)


def splitting(a_ref, high_ref, low_ref):
    high_ref[...], low_ref[...] = split(a_ref[...])


def product(ah, al, m):
    mh, ml = split(m)
    width = m.shape[1]
    first = dot(ah, jnp.concatenate([mh, ml], axis=1), INNER)
    return first[:, :width] + (first[:, width:] + dot(al, mh, INNER))


def products(count, shift_ref, high_ref, low_ref, *refs):
    panels, outs = refs[:count], refs[count:]
    ah, al = high_ref[...], low_ref[...]
    shift = shift_ref[0]
    for i in range(count):
        m = panels[0][...]
        for j in range(1, count):
            m = jnp.where(shift == (i ^ j), panels[j][...], m)
        outs[i][...] = product(ah, al, m)


def pair(same_ref, high_ref, low_ref, mine_ref, other_ref, *outs):
    ah, al = high_ref[...], low_ref[...]
    same = same_ref[0] == 1
    mine, other = mine_ref[...], other_ref[...]
    for m, refs in (
        (jnp.where(same, mine, other), outs[: len(outs) // 2]),
        (jnp.where(same, other, mine), outs[len(outs) // 2 :]),
    ):
        out = product(ah, al, m)
        tall = out.shape[0] // len(refs)
        for i, ref in enumerate(refs):
            ref[...] = out[i * tall : (i + 1) * tall, :]


def finish(width, mask_ref, masked_ref, *refs):
    parts, g_ref, quad_ref = refs[:-2], refs[-2], refs[-1]
    rows = g_ref.shape[0]
    supers, blocks = mask_ref.shape
    tall = rows // blocks
    for b in range(blocks):
        for s in range(supers):
            cols = slice(s * width, (s + 1) * width)
            total = None
            for whole in parts:
                pieces = whole if isinstance(whole, tuple) else (whole,)
                depth = rows // len(pieces)
                ref, at = pieces[b * tall // depth], b * tall % depth
                term = ref[at : at + tall, cols]
                total = term if total is None else total + term
            g_ref[b * tall : (b + 1) * tall, cols] = total * -mask_ref[s, b].astype(F32)
    for s in range(supers):
        cols = slice(s * width, (s + 1) * width)
        mh, ml = split(masked_ref[:, cols])
        gh, gl = split(g_ref[:, cols])
        quad_ref[cols, :] = -(dot(mh, gh, ROWS) + (dot(mh, gl, ROWS) + dot(ml, gh, ROWS)))


def finish_paired(width, mask_ref, masked_ref, own, near, far0, far1, g_ref, quad_ref):
    finish(width, mask_ref, masked_ref, own, near, (far0, far1), g_ref, quad_ref)


def gather_any(side, masked, halves, swap):
    rows, cols = masked.shape
    turned = lax.ppermute(
        masked, GRID, [(r * side + c, c * side + r) for r in range(side) for c in range(side)]
    )
    turned, *halves = lax.optimization_barrier((turned, *halves))
    panels = {0: turned}
    bit = side // 2
    while bit:
        for j, x in list(panels.items()):
            panels[j ^ bit] = swap(x, "row", bit)
        bit //= 2
    shift = jnp.bitwise_xor(lax.axis_index("row"), lax.axis_index("col"))
    partials = call(
        functools.partial(products, side),
        [SMEM] + [VMEM] * (2 + side),
        [((rows, cols), F32)] * side,
        (shift.astype(jnp.int32).reshape(1), *halves, *[panels[j] for j in range(side)]),
        48,
        "products",
    )
    return [partials[0]] + [swap(partials[i], "col", i) for i in range(1, side)]


def route(rule):
    pairs = []
    for x in range(2):
        for t in range(2):
            for h in range(2):
                for l in range(2):
                    to = rule(x, t, h, l)
                    if to is not None:
                        (x2, t2), z2 = to
                        pairs.append((8 * x + 4 * t + 2 * h + l, 8 * x2 + 4 * t2 + z2))
    return pairs


def to_plane(x, t, h, l):
    return ((1 - h, t), 2 * h + l) if t == l else ((1 - h, 1 - t), 2 * h + t)


def cross_early(x, t, h, l):
    return to_plane(x, t, h, l) if x == h else ((1 - x, t), 2 * h + l)


def far_direct(x, t, h, l):
    return to_plane(x, t, h, l) if x == h else ((x, l), 2 * x + t)


def far_both(x, t, h, l):
    return ((x, l), 2 * (1 - x) + t) if x == h else ((x, l), 2 * x + t)


def near_here(x, t, h, l):
    if x != h:
        return None
    return ((x, t), 2 * h + l) if t == l else ((x, 1 - t), 2 * h + t)


def cross_late(x, t, h, l):
    return ((1 - x, t), 2 * h + l) if x == h else None


def gather_four(masked, top, low, inverse_blocks, halved, swap):
    rows, cols = masked.shape
    row, col = lax.axis_index("row"), lax.axis_index("col")
    near_side = (row // 2) == (col // 2)
    same = ((row % 2) == (col % 2)).astype(jnp.int32).reshape(1)

    low_crossed = lax.ppermute(low, GRID, route(cross_early))
    top_moved = lax.ppermute(top, GRID, route(far_direct))
    low_next = jnp.where(near_side, low_crossed, low)
    low_moved = lax.ppermute(low_next, GRID, route(far_both))
    near = lax.ppermute(lax.optimization_barrier((masked, low_next))[0], GRID, route(near_here))
    halves = halved(lax.optimization_barrier((inverse_blocks, low_next))[0])
    top_next, *halves = lax.optimization_barrier((top_moved, *halves))
    top_crossed = lax.ppermute(top_next, GRID, route(cross_late))
    far = jnp.concatenate([jnp.where(near_side, top_moved, top_crossed), low_moved])
    near = jnp.where(near_side, near, jnp.concatenate([top_moved, low_crossed]))
    far_other = swap(far, "row", 1)
    near_other = swap(near, "row", 1)

    half = ((rows // 2, cols), F32)
    far2a, far2b, far3a, far3b = call(
        pair, [SMEM] + [VMEM] * 4, [half] * 4, (same, *halves, far, far_other), 12, "far_pair"
    )
    own, near1 = call(
        pair,
        [SMEM] + [VMEM] * 4,
        [((rows, cols), F32)] * 2,
        (same, *halves, near, near_other),
        12,
        "near_pair",
    )
    first = swap(far3a, "col", 1)
    second = swap(far3b, "col", 1)
    near1 = swap(near1, "col", 1)
    return [own, near1, swap(far2a + first, "col", 2), swap(far2b + second, "col", 2)]


def on_device(side, inverse_blocks, lower_panel, struct_mask, diag_inverse):
    width = diag_inverse.shape[1]
    rows, cols = lower_panel.shape

    def swap(x, axis, bit):
        return lax.ppermute(x, axis, [(i, i ^ bit) for i in range(side)])

    mask = struct_mask.T
    blocks = struct_mask.shape[0]
    four = side == 4 and blocks % 2 == 0

    def masked_rows(*spans):
        return call(
            functools.partial(masking, spans),
            [SMEM, VMEM],
            [((rows * (last - first) // blocks, cols), F32) for first, last in spans],
            (mask, lower_panel),
            4,
            "masking",
        )

    def halved(matrix):
        return call(
            splitting,
            [VMEM],
            [(matrix.shape, jnp.bfloat16)] * 2,
            (matrix,),
            8,
            "splitting",
            20_000_000_000,
        )

    if four:
        (low,) = masked_rows((blocks // 2, blocks))
        masked, top = masked_rows((0, blocks), (0, blocks // 2))
        arrived, body = gather_four(masked, top, low, inverse_blocks, halved, swap), finish_paired
    else:
        (masked,) = masked_rows((0, blocks))
        arrived, body = gather_any(side, masked, halved(inverse_blocks), swap), finish

    g_panel, quad = call(
        functools.partial(body, width),
        [SMEM] + [VMEM] * (1 + len(arrived)),
        [((rows, cols), F32), ((cols, width), F32)],
        (mask, masked, *arrived),
        16,
        "finish",
    )
    bit = 1
    while bit < side:
        quad = quad + swap(quad, "row", bit)
        bit *= 2
    return g_panel, diag_inverse + quad


def solution(mesh):
    side = mesh.shape["row"]
    assert side == mesh.shape["col"] and side & (side - 1) == 0
    placed = (
        P(("pole", "row"), "col"),
        P(("pole", "row"), "col"),
        P("row", "col"),
        P(("pole", "col"), None),
    )
    return jax.shard_map(
        functools.partial(on_device, side),
        mesh=mesh,
        in_specs=placed,
        out_specs=(P(("pole", "row"), "col"), P(("pole", "col"), None)),
        check_vma=False,
    )
```

```python
import functools

import jax
import jax.numpy as jnp
from jax import lax
from jax.experimental import pallas as pl
from jax.experimental.pallas import tpu as pltpu
from jax.sharding import PartitionSpec as P

GRID = ("row", "col")
VMEM = pl.BlockSpec(memory_space=pltpu.VMEM)
SMEM = pl.BlockSpec(memory_space=pltpu.SMEM)
HBM = pl.BlockSpec(memory_space=pltpu.HBM)
F32 = jnp.float32
ROWS = ((0,), (0,))
INNER = ((1,), (0,))


def split(x):
    high = x.astype(jnp.bfloat16)
    return high, (x - high.astype(F32)).astype(jnp.bfloat16)


def dot(a, b, dims):
    return lax.dot_general(a, b, (dims, ((), ())), preferred_element_type=F32)


def call(body, ins, outs, args, grant, name, flops=None, scratch=()):
    return pl.pallas_call(
        body,
        out_shape=[jax.ShapeDtypeStruct(shape, dtype) for shape, dtype in outs],
        in_specs=ins,
        out_specs=[VMEM] * len(outs),
        scratch_shapes=scratch,
        compiler_params=pltpu.CompilerParams(vmem_limit_bytes=grant << 20),
        cost_estimate=flops
        and pl.CostEstimate(flops=flops, bytes_accessed=0, transcendentals=0),
        name=name,
    )(*args)


def fold(x):
    tall = x.shape[0] // 2
    return jnp.concatenate([x[:tall], x[tall:]], axis=1)


def unfold(x):
    wide = x.shape[1] // 2
    return jnp.concatenate([x[:, :wide], x[:, wide:]], axis=0)


def masked_part(mask_ref, panel_ref, cols):
    supers, blocks = mask_ref.shape
    tall, wide = panel_ref.shape[0] // blocks, panel_ref.shape[1] // supers
    rows = []
    for b in range(blocks):
        at = slice(b * tall, (b + 1) * tall)
        row = [
            panel_ref[at, s * wide : (s + 1) * wide] * mask_ref[s, b].astype(F32)
            for s in range(supers)
        ]
        rows.append((row[0] if supers == 1 else jnp.concatenate(row, axis=1))[:, cols])
    return jnp.concatenate(rows, axis=0)


def masking(mask_ref, panel_ref, out_ref):
    out_ref[...] = masked_part(mask_ref, panel_ref, slice(None))


def masking_first(mask_hbm, panel_hbm, first_ref, mask_ref, panel_ref, sems):
    rows = panel_ref.shape[0] // 4
    copies = [pltpu.make_async_copy(mask_hbm, mask_ref, sems.at[4])]
    for i in range(4):
        at = pl.ds(i * rows, rows)
        copies.append(pltpu.make_async_copy(panel_hbm.at[at], panel_ref.at[at], sems.at[i]))
    for copy in copies:
        copy.start()
    for copy in copies:
        copy.wait()
    first_ref[...] = fold(masked_part(mask_ref, panel_ref, slice(0, panel_ref.shape[1] // 2)))


def masking_rest(mask_ref, panel_ref, out_ref, second_ref):
    whole = masked_part(mask_ref, panel_ref, slice(None))
    out_ref[...] = whole
    second_ref[...] = fold(whole[:, panel_ref.shape[1] // 2 :])


def splitting(a_ref, high_ref, low_ref):
    high_ref[...], low_ref[...] = split(a_ref[...])


def product(ah, al, m):
    mh, ml = split(m)
    width = m.shape[1]
    first = dot(ah, jnp.concatenate([mh, ml], axis=1), INNER)
    return first[:, :width] + (first[:, width:] + dot(al, mh, INNER))


def products(count, shift_ref, high_ref, low_ref, *refs):
    panels, outs = refs[:count], refs[count:]
    ah, al = high_ref[...], low_ref[...]
    shift = shift_ref[0]
    for i in range(count):
        m = panels[0][...]
        for j in range(1, count):
            m = jnp.where(shift == (i ^ j), panels[j][...], m)
        outs[i][...] = product(ah, al, m)


def near_pair(same_ref, high_ref, low_ref, mine_ref, other_ref, own_ref, next_ref):
    same = same_ref[0] == 1
    mine, other = mine_ref[...], other_ref[...]
    ah, al = high_ref[...], low_ref[...]
    next_ref[...] = product(ah, al, jnp.where(same, other, mine))
    own_ref[...] = product(ah, al, jnp.where(same, mine, other))


def far_pair(same_ref, high_ref, low_ref, mine_ref, other_ref, two_ref, three_ref):
    same = same_ref[0] == 1
    mine, other = unfold(mine_ref[...]), unfold(other_ref[...])
    two, three = jnp.where(same, mine, other), jnp.where(same, other, mine)
    out = product(high_ref[...], low_ref[...], jnp.concatenate([two, three], axis=1))
    wide = two.shape[1]
    two_ref[...], three_ref[...] = fold(out[:, :wide]), fold(out[:, wide:])


def finish_sum(width, mask_ref, masked_ref, total, g_ref, quad_ref):
    supers, blocks = mask_ref.shape
    tall = total.shape[0] // blocks
    for b in range(blocks):
        for s in range(supers):
            at = (slice(b * tall, (b + 1) * tall), slice(s * width, (s + 1) * width))
            g_ref[at] = total[at] * -mask_ref[s, b].astype(F32)
    for s in range(supers):
        cols = slice(s * width, (s + 1) * width)
        mh, ml = split(masked_ref[:, cols])
        gh, gl = split(g_ref[:, cols])
        quad_ref[cols, :] = -(dot(mh, gh, ROWS) + (dot(mh, gl, ROWS) + dot(ml, gh, ROWS)))


def finish(width, mask_ref, masked_ref, *refs):
    total = refs[0][...]
    for ref in refs[1:-2]:
        total = total + ref[...]
    finish_sum(width, mask_ref, masked_ref, total, *refs[-2:])


def finish_folded(width, mask_ref, masked_ref, own, near, far0, far1, g_ref, quad_ref):
    far = jnp.concatenate([unfold(far0[...]), unfold(far1[...])], axis=1)
    finish_sum(width, mask_ref, masked_ref, own[...] + near[...] + far, g_ref, quad_ref)


def gather_any(side, masked, halves, swap):
    rows, cols = masked.shape
    turned = lax.ppermute(
        masked, GRID, [(r * side + c, c * side + r) for r in range(side) for c in range(side)]
    )
    turned, *halves = lax.optimization_barrier((turned, *halves))
    panels = {0: turned}
    bit = side // 2
    while bit:
        for j, x in list(panels.items()):
            panels[j ^ bit] = swap(x, "row", bit)
        bit //= 2
    shift = jnp.bitwise_xor(lax.axis_index("row"), lax.axis_index("col"))
    partials = call(
        functools.partial(products, side),
        [SMEM] + [VMEM] * (2 + side),
        [((rows, cols), F32)] * side,
        (shift.astype(jnp.int32).reshape(1), *halves, *[panels[j] for j in range(side)]),
        48,
        "products",
    )
    return [partials[0]] + [swap(partials[i], "col", i) for i in range(1, side)]


def route(rule):
    pairs = []
    for x in range(2):
        for t in range(2):
            for h in range(2):
                for l in range(2):
                    to = rule(x, t, h, l)
                    if to is not None:
                        (x2, t2), z2 = to
                        pairs.append((8 * x + 4 * t + 2 * h + l, 8 * x2 + 4 * t2 + z2))
    return pairs


def cross_early(x, t, h, l):
    return ((1 - x, t), 2 * h + l) if x != h else None


def far_direct(x, t, h, l):
    return ((x, l), 2 * x + t) if x != h else None


def far_crossed(x, t, h, l):
    return ((x, l), 2 * (1 - x) + t) if x == h else None


def cross_late(x, t, h, l):
    return ((1 - x, t), 2 * h + l) if x == h else None


def near_here(x, t, h, l):
    if x != h:
        return None
    return ((x, t), 2 * h + l) if t == l else ((x, 1 - t), 2 * h + t)


def near_across(x, t, h, l):
    if x != h:
        return None
    return ((1 - x, t), 2 * h + l) if t == l else ((1 - x, 1 - t), 2 * h + t)


def move(x, rule, name):
    with jax.named_scope(name):
        return lax.ppermute(x, GRID, route(rule))


def after(x, *others):
    return lax.optimization_barrier((x, *others))[0]


def gather_four(first, rest, panel, matrix, halved, swap):
    row, col = lax.axis_index("row"), lax.axis_index("col")
    near_side = (row // 2) == (col // 2)
    same = ((row % 2) == (col % 2)).astype(jnp.int32).reshape(1)
    half, whole = (first.shape, F32), (panel.shape, F32)

    crossing = move(first, cross_early, "cross0")
    direct0 = move(first, far_direct, "direct0")
    crossed0 = move(crossing, far_crossed, "crossed0")
    masked, second = rest(after(panel, first))
    direct1 = move(second, far_direct, "direct1")
    halves = halved(after(matrix, crossing))

    def partials(mine, name):
        return call(
            far_pair,
            [SMEM] + [VMEM] * 4,
            [half] * 2,
            (same, *halves, mine, swap(mine, "row", 1, name)),
            12,
            "far_pair",
        )

    mine0 = jnp.where(near_side, direct0, crossed0)
    two0, three0 = partials(mine0, "cores0")
    sum0 = two0 + swap(three0, "col", 1, "next0")
    direct1 = after(direct1, three0)
    mine1 = jnp.where(near_side, direct1, move(direct1, cross_late, "cross1"))
    two1, three1 = partials(after(mine1, sum0), "cores1")
    far0 = swap(sum0, "col", 2, "across0")
    sum1 = two1 + swap(three1, "col", 1, "next1")
    far1 = swap(sum1, "col", 2, "across1")
    near_panel = after(masked, direct0)
    near_mine = jnp.where(
        near_side,
        move(near_panel, near_here, "near_here"),
        move(near_panel, near_across, "near_across"),
    )
    own, near1 = call(
        near_pair,
        [SMEM] + [VMEM] * 4,
        [whole] * 2,
        (same, *halves, near_mine, swap(near_mine, "row", 1, "near_cores")),
        12,
        "near_pair",
    )
    near1 = swap(after(near1, sum0), "col", 1, "near_partial")
    return [own, near1, far0, far1, masked]


def on_device(side, inverse_blocks, lower_panel, struct_mask, diag_inverse):
    width = diag_inverse.shape[1]
    rows, cols = lower_panel.shape

    def swap(x, axis, bit, name="swap"):
        with jax.named_scope(name):
            return lax.ppermute(x, axis, [(i, i ^ bit) for i in range(side)])

    mask = struct_mask.T
    blocks = struct_mask.shape[0]
    four = side == 4 and blocks % 2 == 0

    whole, half = ((rows, cols), F32), ((rows // 2, cols), F32)

    def mask_panel(body, outs, panel):
        return call(body, [SMEM, VMEM], outs, (mask, panel), 4, "masking")

    def halved(matrix):
        return call(
            splitting,
            [VMEM],
            [(matrix.shape, jnp.bfloat16)] * 2,
            (matrix,),
            8,
            "splitting",
            20_000_000_000,
        )

    if four:
        (first,) = call(
            masking_first,
            [HBM, HBM],
            [half],
            (mask, lower_panel),
            4,
            "masking_first",
            scratch=[
                pltpu.SMEM(mask.shape, mask.dtype),
                pltpu.VMEM((rows, cols), F32),
                pltpu.SemaphoreType.DMA((5,)),
            ],
        )
        rest = functools.partial(mask_panel, masking_rest, [whole, half])
        arrived = gather_four(first, rest, lower_panel, inverse_blocks, halved, swap)
        masked = arrived.pop()
        body = finish_folded
    else:
        (masked,) = mask_panel(masking, [whole], lower_panel)
        arrived, body = gather_any(side, masked, halved(inverse_blocks), swap), finish

    g_panel, quad = call(
        functools.partial(body, width),
        [SMEM] + [VMEM] * (1 + len(arrived)),
        [((rows, cols), F32), ((cols, width), F32)],
        (mask, masked, *arrived),
        16,
        "finish",
    )
    bit = 1
    while bit < side:
        quad = quad + swap(quad, "row", bit)
        bit *= 2
    return g_panel, diag_inverse + quad


def solution(mesh):
    side = mesh.shape["row"]
    assert side == mesh.shape["col"] and side & (side - 1) == 0
    placed = (
        P(("pole", "row"), "col"),
        P(("pole", "row"), "col"),
        P("row", "col"),
        P(("pole", "col"), None),
    )
    return jax.shard_map(
        functools.partial(on_device, side),
        mesh=mesh,
        in_specs=placed,
        out_specs=(P(("pole", "row"), "col"), P(("pole", "col"), None)),
        check_vma=False,
    )
```

```python
import functools

import jax
import jax.numpy as jnp
from jax import lax
from jax.experimental import pallas as pl
from jax.experimental.pallas import tpu as pltpu
from jax.sharding import PartitionSpec as P

GRID = ("row", "col")
VMEM = pl.BlockSpec(memory_space=pltpu.VMEM)
SMEM = pl.BlockSpec(memory_space=pltpu.SMEM)
F32 = jnp.float32
ROWS = ((0,), (0,))
INNER = ((1,), (0,))


def split(x):
    high = x.astype(jnp.bfloat16)
    return high, (x - high.astype(F32)).astype(jnp.bfloat16)


def dot(a, b, dims):
    return lax.dot_general(a, b, (dims, ((), ())), preferred_element_type=F32)


def call(body, ins, outs, args, grant, name, flops=None):
    return pl.pallas_call(
        body,
        out_shape=[jax.ShapeDtypeStruct(shape, dtype) for shape, dtype in outs],
        in_specs=ins,
        out_specs=[VMEM] * len(outs),
        compiler_params=pltpu.CompilerParams(vmem_limit_bytes=grant << 20),
        cost_estimate=flops
        and pl.CostEstimate(flops=flops, bytes_accessed=0, transcendentals=0),
        name=name,
    )(*args)


def masking(mask_ref, panel_ref, out_ref):
    supers, blocks = mask_ref.shape
    tall, wide = panel_ref.shape[0] // blocks, panel_ref.shape[1] // supers
    for b in range(blocks):
        for s in range(supers):
            at = (slice(b * tall, (b + 1) * tall), slice(s * wide, (s + 1) * wide))
            out_ref[at] = panel_ref[at] * mask_ref[s, b].astype(F32)


def splitting(a_ref, high_ref, low_ref):
    high_ref[...], low_ref[...] = split(a_ref[...])


def product(ah, al, m):
    mh, ml = split(m)
    width = m.shape[1]
    first = dot(ah, jnp.concatenate([mh, ml], axis=1), INNER)
    return first[:, :width] + (first[:, width:] + dot(al, mh, INNER))


def products(count, shift_ref, high_ref, low_ref, *refs):
    panels, outs = refs[:count], refs[count:]
    ah, al = high_ref[...], low_ref[...]
    shift = shift_ref[0]
    for i in range(count):
        m = panels[0][...]
        for j in range(1, count):
            m = jnp.where(shift == (i ^ j), panels[j][...], m)
        outs[i][...] = product(ah, al, m)


def block_product(high_ref, low_ref, held_ref, sent_ref, out_ref):
    out_ref[...] = product(high_ref[...], low_ref[...], held_ref[...] + sent_ref[...])


def finish(width, mask_ref, masked_ref, *refs):
    parts, g_ref, quad_ref = refs[:-2], refs[-2], refs[-1]
    total = parts[0][...]
    for part in parts[1:]:
        total = total + part[...]
    supers, blocks = mask_ref.shape
    tall = total.shape[0] // blocks
    for b in range(blocks):
        for s in range(supers):
            at = (slice(b * tall, (b + 1) * tall), slice(s * width, (s + 1) * width))
            g_ref[at] = total[at] * -mask_ref[s, b].astype(F32)
    for s in range(supers):
        cols = slice(s * width, (s + 1) * width)
        mh, ml = split(masked_ref[:, cols])
        gh, gl = split(g_ref[:, cols])
        quad_ref[cols, :] = -(dot(mh, gh, ROWS) + (dot(mh, gl, ROWS) + dot(ml, gh, ROWS)))


def gather_any(side, masked, halves, swap):
    rows, cols = masked.shape
    turned = lax.ppermute(
        masked, GRID, [(r * side + c, c * side + r) for r in range(side) for c in range(side)]
    )
    turned, *halves = lax.optimization_barrier((turned, *halves))
    panels = {0: turned}
    bit = side // 2
    while bit:
        for j, x in list(panels.items()):
            panels[j ^ bit] = swap(x, "row", bit)
        bit //= 2
    shift = jnp.bitwise_xor(lax.axis_index("row"), lax.axis_index("col"))
    partials = call(
        functools.partial(products, side),
        [SMEM] + [VMEM] * (2 + side),
        [((rows, cols), F32)] * side,
        (shift.astype(jnp.int32).reshape(1), *halves, *[panels[j] for j in range(side)]),
        48,
        "products",
    )
    return [partials[0]] + [swap(partials[i], "col", i) for i in range(1, side)]


def move(x, name, pairs):
    with jax.named_scope(name):
        return lax.ppermute(x, GRID, [(4 * r + c, 4 * r2 + c2) for (r, c), (r2, c2) in pairs])


def after(x, *others):
    return lax.optimization_barrier((x, *others))[0]


def pinned(x_ref, out_ref):
    del x_ref, out_ref


def pin(x, flops):
    return pl.pallas_call(
        pinned,
        out_shape=jax.ShapeDtypeStruct(x.shape, x.dtype),
        in_specs=[VMEM],
        out_specs=VMEM,
        input_output_aliases={0: 0},
        compiler_params=pltpu.CompilerParams(vmem_limit_bytes=4 << 20),
        cost_estimate=pl.CostEstimate(flops=flops, bytes_accessed=1, transcendentals=0),
        name="pinned",
    )(x)


def gather_four(masked, matrix, halved, swap):
    root = lax.axis_index("row") == lax.axis_index("col")

    def to_root(x, j):
        return move(x, f"root{j}", [((r, r ^ j), (r, r)) for r in range(4)])

    def cross(x, j):
        return move(x, f"cross{j}", [((r, r), (r ^ 2, r)) for r in range(4)])

    def cores(x, j):
        return move(x, f"cores{j}", [((r ^ i, r), (r ^ i ^ 1, r)) for r in range(4) for i in (0, 2)])

    def partial(held, j):
        return call(
            block_product,
            [VMEM] * 4,
            [(held.shape, F32)],
            (*halves, held, cores(held, j)),
            8,
            f"block{j}",
        )[0]

    root3 = to_root(masked, 3)
    root2 = to_root(masked, 2)
    halves = halved(after(matrix, masked))
    held3 = root3 + cross(root3, 3)
    three = partial(held3, 3)
    first = swap(three, "col", 1, "first")
    root2 = pin(root2, 5_000_000_000)
    root2 = after(root2, three)
    held2 = root2 + cross(root2, 2)
    two = partial(held2, 2)
    total = two + pin(first, 50_000_000_000)
    far = pin(swap(total, "col", 2, "second"), 5_000_000_000)
    near_panel = after(masked, *halves)
    root1 = pin(to_root(near_panel, 1), 5_000_000_000)
    one = partial(root1 + cross(after(root1, held2), 1), 1)
    near = swap(after(one, total), "col", 1, "near")
    own = partial(jnp.where(root, masked, pin(cross(after(masked, *halves), 0), 5_000_000_000)), 0)
    return [own, near, far]


def on_device(side, inverse_blocks, lower_panel, struct_mask, diag_inverse):
    width = diag_inverse.shape[1]
    rows, cols = lower_panel.shape

    def swap(x, axis, bit, name="swap"):
        with jax.named_scope(name):
            return lax.ppermute(x, axis, [(i, i ^ bit) for i in range(side)])

    mask = struct_mask.T
    whole = ((rows, cols), F32)
    (masked,) = call(masking, [SMEM, VMEM], [whole], (mask, lower_panel), 4, "masking")

    def halved(matrix):
        return call(
            splitting,
            [VMEM],
            [(matrix.shape, jnp.bfloat16)] * 2,
            (matrix,),
            8,
            "splitting",
            20_000_000_000,
        )

    if side == 4:
        arrived = gather_four(masked, inverse_blocks, halved, swap)
    else:
        arrived = gather_any(side, masked, halved(inverse_blocks), swap)

    g_panel, quad = call(
        functools.partial(finish, width),
        [SMEM] + [VMEM] * (1 + len(arrived)),
        [whole, ((cols, width), F32)],
        (mask, masked, *arrived),
        16,
        "finish",
    )
    bit = 1
    while bit < side:
        quad = quad + swap(quad, "row", bit)
        bit *= 2
    return g_panel, diag_inverse + quad


def solution(mesh):
    side = mesh.shape["row"]
    assert side == mesh.shape["col"] and side & (side - 1) == 0
    placed = (
        P(("pole", "row"), "col"),
        P(("pole", "row"), "col"),
        P("row", "col"),
        P(("pole", "col"), None),
    )
    return jax.shard_map(
        functools.partial(on_device, side),
        mesh=mesh,
        in_specs=placed,
        out_specs=(P(("pole", "row"), "col"), P(("pole", "col"), None)),
        check_vma=False,
    )
```

```python
import functools

import jax
import jax.numpy as jnp
from jax import lax
from jax.experimental import pallas as pl
from jax.experimental.pallas import tpu as pltpu
from jax.sharding import PartitionSpec as P

GRID = ("row", "col")
VMEM = pl.BlockSpec(memory_space=pltpu.VMEM)
SMEM = pl.BlockSpec(memory_space=pltpu.SMEM)
F32 = jnp.float32
ROWS = ((0,), (0,))
INNER = ((1,), (0,))


def split(x):
    high = x.astype(jnp.bfloat16)
    return high, (x - high.astype(F32)).astype(jnp.bfloat16)


def dot(a, b, dims):
    return lax.dot_general(a, b, (dims, ((), ())), preferred_element_type=F32)


def call(body, ins, outs, args, grant, name, flops=None):
    return pl.pallas_call(
        body,
        out_shape=[jax.ShapeDtypeStruct(shape, dtype) for shape, dtype in outs],
        in_specs=ins,
        out_specs=[VMEM] * len(outs),
        compiler_params=pltpu.CompilerParams(vmem_limit_bytes=grant << 20),
        cost_estimate=flops
        and pl.CostEstimate(flops=flops, bytes_accessed=0, transcendentals=0),
        name=name,
    )(*args)


def masking(spans, mask_ref, panel_ref, *out_refs):
    supers, blocks = mask_ref.shape
    tall, wide = panel_ref.shape[0] // blocks, panel_ref.shape[1] // supers
    for (first, last), ref in zip(spans, out_refs):
        for b in range(first, last):
            for s in range(supers):
                cols = slice(s * wide, (s + 1) * wide)
                block = panel_ref[b * tall : (b + 1) * tall, cols]
                at = (b - first) * tall
                ref[at : at + tall, cols] = block * mask_ref[s, b].astype(F32)


def splitting(a_ref, high_ref, low_ref):
    high_ref[...], low_ref[...] = split(a_ref[...])


def product(ah, al, m):
    mh, ml = split(m)
    width = m.shape[1]
    first = dot(ah, jnp.concatenate([mh, ml], axis=1), INNER)
    return first[:, :width] + (first[:, width:] + dot(al, mh, INNER))


def products(count, shift_ref, high_ref, low_ref, *refs):
    panels, outs = refs[:count], refs[count:]
    ah, al = high_ref[...], low_ref[...]
    shift = shift_ref[0]
    for i in range(count):
        m = panels[0][...]
        for j in range(1, count):
            m = jnp.where(shift == (i ^ j), panels[j][...], m)
        outs[i][...] = product(ah, al, m)


def pair(same_ref, high_ref, low_ref, mine_ref, other_ref, *outs):
    ah, al = high_ref[...], low_ref[...]
    same = same_ref[0] == 1
    mine, other = mine_ref[...], other_ref[...]
    for m, refs in (
        (jnp.where(same, mine, other), outs[: len(outs) // 2]),
        (jnp.where(same, other, mine), outs[len(outs) // 2 :]),
    ):
        out = product(ah, al, m)
        tall = out.shape[0] // len(refs)
        for i, ref in enumerate(refs):
            ref[...] = out[i * tall : (i + 1) * tall, :]


def finish(width, mask_ref, masked_ref, *refs):
    parts, g_ref, quad_ref = refs[:-2], refs[-2], refs[-1]
    rows = g_ref.shape[0]
    supers, blocks = mask_ref.shape
    tall = rows // blocks
    for b in range(blocks):
        for s in range(supers):
            cols = slice(s * width, (s + 1) * width)
            total = None
            for whole in parts:
                pieces = whole if isinstance(whole, tuple) else (whole,)
                depth = rows // len(pieces)
                ref, at = pieces[b * tall // depth], b * tall % depth
                term = ref[at : at + tall, cols]
                total = term if total is None else total + term
            g_ref[b * tall : (b + 1) * tall, cols] = total * -mask_ref[s, b].astype(F32)
    for s in range(supers):
        cols = slice(s * width, (s + 1) * width)
        mh, ml = split(masked_ref[:, cols])
        gh, gl = split(g_ref[:, cols])
        quad_ref[cols, :] = -(dot(mh, gh, ROWS) + (dot(mh, gl, ROWS) + dot(ml, gh, ROWS)))


def finish_paired(width, mask_ref, masked_ref, own, near, far0, far1, g_ref, quad_ref):
    finish(width, mask_ref, masked_ref, own, near, (far0, far1), g_ref, quad_ref)


def gather_any(side, masked, halves, swap):
    rows, cols = masked.shape
    turned = lax.ppermute(
        masked, GRID, [(r * side + c, c * side + r) for r in range(side) for c in range(side)]
    )
    turned, *halves = lax.optimization_barrier((turned, *halves))
    panels = {0: turned}
    bit = side // 2
    while bit:
        for j, x in list(panels.items()):
            panels[j ^ bit] = swap(x, "row", bit)
        bit //= 2
    shift = jnp.bitwise_xor(lax.axis_index("row"), lax.axis_index("col"))
    partials = call(
        functools.partial(products, side),
        [SMEM] + [VMEM] * (2 + side),
        [((rows, cols), F32)] * side,
        (shift.astype(jnp.int32).reshape(1), *halves, *[panels[j] for j in range(side)]),
        48,
        "products",
    )
    return [partials[0]] + [swap(partials[i], "col", i) for i in range(1, side)]


def route(rule):
    pairs = []
    for x in range(2):
        for t in range(2):
            for h in range(2):
                for l in range(2):
                    to = rule(x, t, h, l)
                    if to is not None:
                        (x2, t2), z2 = to
                        pairs.append((8 * x + 4 * t + 2 * h + l, 8 * x2 + 4 * t2 + z2))
    return pairs


def to_plane(x, t, h, l):
    return ((1 - h, t), 2 * h + l) if t == l else ((1 - h, 1 - t), 2 * h + t)


def cross_early(x, t, h, l):
    return to_plane(x, t, h, l) if x == h else ((1 - x, t), 2 * h + l)


def far_direct(x, t, h, l):
    return to_plane(x, t, h, l) if x == h else ((x, l), 2 * x + t)


def far_both(x, t, h, l):
    return ((x, l), 2 * (1 - x) + t) if x == h else ((x, l), 2 * x + t)


def near_here(x, t, h, l):
    if x != h:
        return None
    return ((x, t), 2 * h + l) if t == l else ((x, 1 - t), 2 * h + t)


def cross_late(x, t, h, l):
    return ((1 - x, t), 2 * h + l) if x == h else None


def pinned(x_ref, out_ref):
    del x_ref, out_ref


def pin(x, flops):
    return pl.pallas_call(
        pinned,
        out_shape=jax.ShapeDtypeStruct(x.shape, x.dtype),
        in_specs=[VMEM],
        out_specs=VMEM,
        input_output_aliases={0: 0},
        compiler_params=pltpu.CompilerParams(vmem_limit_bytes=4 << 20),
        cost_estimate=pl.CostEstimate(flops=flops, bytes_accessed=1, transcendentals=0),
        name="pinned",
    )(x)


def move(x, rule, name):
    with jax.named_scope(name):
        return lax.ppermute(x, GRID, route(rule))


def after(x, *others):
    return lax.optimization_barrier((x, *others))[0]


def gather_four(masked, top, low, inverse_blocks, halved, swap):
    rows, cols = masked.shape
    row, col = lax.axis_index("row"), lax.axis_index("col")
    near_side = (row // 2) == (col // 2)
    same = ((row % 2) == (col % 2)).astype(jnp.int32).reshape(1)

    low_crossed = move(low, cross_early, "low_crossed")
    top_moved = move(top, far_direct, "top_moved")
    low_next = jnp.where(near_side, low_crossed, low)
    low_moved = pin(move(low_next, far_both, "low_moved"), 100_000_000_000)
    near = move(after(masked, low_next), near_here, "near_here")
    halves = halved(after(inverse_blocks, low_next))
    top_next = after(top_moved, *halves)
    top_crossed = move(top_next, cross_late, "top_crossed")
    far = jnp.concatenate([jnp.where(near_side, top_moved, top_crossed), low_moved])
    near = jnp.where(near_side, near, jnp.concatenate([top_moved, low_crossed]))
    far_other = swap(far, "row", 1, "far_cores")
    near_other = swap(near, "row", 1, "near_cores")

    half = ((rows // 2, cols), F32)
    far2a, far2b, far3a, far3b = call(
        pair, [SMEM] + [VMEM] * 4, [half] * 4, (same, *halves, far, far_other), 12, "far_pair"
    )
    own, near1 = call(
        pair,
        [SMEM] + [VMEM] * 4,
        [((rows, cols), F32)] * 2,
        (same, *halves, near, near_other),
        12,
        "near_pair",
    )
    sum_a = far2a + swap(far3a, "col", 1, "next_a")
    sum_b = far2b + swap(far3b, "col", 1, "next_b")
    far_a = pin(swap(sum_a, "col", 2, "across_a"), 3_000_000_000)
    far_b = swap(sum_b, "col", 2, "across_b")
    near1 = swap(after(near1, sum_b), "col", 1, "near_partial")
    return [own, near1, far_a, far_b]


def on_device(side, inverse_blocks, lower_panel, struct_mask, diag_inverse):
    width = diag_inverse.shape[1]
    rows, cols = lower_panel.shape

    def swap(x, axis, bit, name="swap"):
        with jax.named_scope(name):
            return lax.ppermute(x, axis, [(i, i ^ bit) for i in range(side)])

    mask = struct_mask.T
    blocks = struct_mask.shape[0]
    four = side == 4 and blocks % 2 == 0

    def masked_rows(*spans):
        return call(
            functools.partial(masking, spans),
            [SMEM, VMEM],
            [((rows * (last - first) // blocks, cols), F32) for first, last in spans],
            (mask, lower_panel),
            4,
            "masking",
        )

    def halved(matrix):
        return call(
            splitting,
            [VMEM],
            [(matrix.shape, jnp.bfloat16)] * 2,
            (matrix,),
            8,
            "splitting",
            20_000_000_000,
        )

    if four:
        (low,) = masked_rows((blocks // 2, blocks))
        masked, top = masked_rows((0, blocks), (0, blocks // 2))
        arrived, body = gather_four(masked, top, low, inverse_blocks, halved, swap), finish_paired
    else:
        (masked,) = masked_rows((0, blocks))
        arrived, body = gather_any(side, masked, halved(inverse_blocks), swap), finish

    g_panel, quad = call(
        functools.partial(body, width),
        [SMEM] + [VMEM] * (1 + len(arrived)),
        [((rows, cols), F32), ((cols, width), F32)],
        (mask, masked, *arrived),
        16,
        "finish",
    )
    bit = 1
    while bit < side:
        quad = quad + swap(quad, "row", bit)
        bit *= 2
    return g_panel, diag_inverse + quad


def solution(mesh):
    side = mesh.shape["row"]
    assert side == mesh.shape["col"] and side & (side - 1) == 0
    placed = (
        P(("pole", "row"), "col"),
        P(("pole", "row"), "col"),
        P("row", "col"),
        P(("pole", "col"), None),
    )
    return jax.shard_map(
        functools.partial(on_device, side),
        mesh=mesh,
        in_specs=placed,
        out_specs=(P(("pole", "row"), "col"), P(("pole", "col"), None)),
        check_vma=False,
    )
```

```python
import functools

import jax
import jax.numpy as jnp
from jax import lax
from jax.experimental import pallas as pl
from jax.experimental.pallas import tpu as pltpu
from jax.sharding import PartitionSpec as P

GRID = ("row", "col")
VMEM = pl.BlockSpec(memory_space=pltpu.VMEM)
SMEM = pl.BlockSpec(memory_space=pltpu.SMEM)
F32 = jnp.float32
ROWS = ((0,), (0,))
INNER = ((1,), (0,))


def split(x):
    high = x.astype(jnp.bfloat16)
    return high, (x - high.astype(F32)).astype(jnp.bfloat16)


def dot(a, b, dims):
    return lax.dot_general(a, b, (dims, ((), ())), preferred_element_type=F32)


def call(body, ins, outs, args, grant, name, flops=None, scratch=()):
    return pl.pallas_call(
        body,
        out_shape=[jax.ShapeDtypeStruct(shape, dtype) for shape, dtype in outs],
        in_specs=ins,
        out_specs=[VMEM] * len(outs),
        scratch_shapes=scratch,
        compiler_params=pltpu.CompilerParams(vmem_limit_bytes=grant << 20),
        cost_estimate=flops
        and pl.CostEstimate(flops=flops, bytes_accessed=0, transcendentals=0),
        name=name,
    )(*args)


def masking(spans, mask_ref, panel_ref, *out_refs):
    supers, blocks = mask_ref.shape
    tall, wide = panel_ref.shape[0] // blocks, panel_ref.shape[1] // supers
    for (first, last), ref in zip(spans, out_refs):
        for b in range(first, last):
            for s in range(supers):
                cols = slice(s * wide, (s + 1) * wide)
                block = panel_ref[b * tall : (b + 1) * tall, cols]
                at = (b - first) * tall
                ref[at : at + tall, cols] = block * mask_ref[s, b].astype(F32)


def splitting(a_ref, high_ref, low_ref):
    high_ref[...], low_ref[...] = split(a_ref[...])


def product(ah, al, m):
    mh, ml = split(m)
    width = m.shape[1]
    first = dot(ah, jnp.concatenate([mh, ml], axis=1), INNER)
    return first[:, :width] + (first[:, width:] + dot(al, mh, INNER))


def products(count, shift_ref, high_ref, low_ref, *refs):
    panels, outs = refs[:count], refs[count:]
    ah, al = high_ref[...], low_ref[...]
    shift = shift_ref[0]
    for i in range(count):
        m = panels[0][...]
        for j in range(1, count):
            m = jnp.where(shift == (i ^ j), panels[j][...], m)
        outs[i][...] = product(ah, al, m)


def pair(same_ref, high_ref, low_ref, mine_ref, other_ref, *outs):
    ah, al = high_ref[...], low_ref[...]
    same = same_ref[0] == 1
    mine, other = mine_ref[...], other_ref[...]
    for m, refs in (
        (jnp.where(same, mine, other), outs[: len(outs) // 2]),
        (jnp.where(same, other, mine), outs[len(outs) // 2 :]),
    ):
        out = product(ah, al, m)
        tall = out.shape[0] // len(refs)
        for i, ref in enumerate(refs):
            ref[...] = out[i * tall : (i + 1) * tall, :]


def finish(width, mask_ref, masked_ref, *refs):
    parts, g_ref, quad_ref = refs[:-2], refs[-2], refs[-1]
    rows = g_ref.shape[0]
    supers, blocks = mask_ref.shape
    tall = rows // blocks
    for b in range(blocks):
        for s in range(supers):
            cols = slice(s * width, (s + 1) * width)
            total = None
            for whole in parts:
                pieces = whole if isinstance(whole, tuple) else (whole,)
                depth = rows // len(pieces)
                ref, at = pieces[b * tall // depth], b * tall % depth
                term = ref[at : at + tall, cols]
                total = term if total is None else total + term
            g_ref[b * tall : (b + 1) * tall, cols] = total * -mask_ref[s, b].astype(F32)
    for s in range(supers if quad_ref is not None else 0):
        cols = slice(s * width, (s + 1) * width)
        mh, ml = split(masked_ref[:, cols])
        gh, gl = split(g_ref[:, cols])
        quad_ref[cols, :] = -(dot(mh, gh, ROWS) + (dot(mh, gl, ROWS) + dot(ml, gh, ROWS)))


def quad_only(width, mask_ref, masked_ref, own, near, *refs):
    *fars, g_ref, quad_ref = refs[:-2] + (refs[-1], refs[-2])
    finish(width, mask_ref, masked_ref, own, near, tuple(fars), g_ref, quad_ref)


def panel_only(width, mask_ref, own, near, *refs):
    finish(width, mask_ref, None, own, near, tuple(refs[:-1]), refs[-1], None)


def gather_any(side, masked, halves, swap):
    rows, cols = masked.shape
    turned = lax.ppermute(
        masked, GRID, [(r * side + c, c * side + r) for r in range(side) for c in range(side)]
    )
    turned, *halves = lax.optimization_barrier((turned, *halves))
    panels = {0: turned}
    bit = side // 2
    while bit:
        for j, x in list(panels.items()):
            panels[j ^ bit] = swap(x, "row", bit)
        bit //= 2
    shift = jnp.bitwise_xor(lax.axis_index("row"), lax.axis_index("col"))
    partials = call(
        functools.partial(products, side),
        [SMEM] + [VMEM] * (2 + side),
        [((rows, cols), F32)] * side,
        (shift.astype(jnp.int32).reshape(1), *halves, *[panels[j] for j in range(side)]),
        48,
        "products",
    )
    return [partials[0]] + [swap(partials[i], "col", i) for i in range(1, side)]


def route(rule):
    pairs = []
    for x in range(2):
        for t in range(2):
            for h in range(2):
                for l in range(2):
                    to = rule(x, t, h, l)
                    if to is not None:
                        (x2, t2), z2 = to
                        pairs.append((8 * x + 4 * t + 2 * h + l, 8 * x2 + 4 * t2 + z2))
    return pairs


def to_plane(x, t, h, l):
    return ((1 - h, t), 2 * h + l) if t == l else ((1 - h, 1 - t), 2 * h + t)


def cross_early(x, t, h, l):
    return to_plane(x, t, h, l) if x == h else ((1 - x, t), 2 * h + l)


def far_direct(x, t, h, l):
    return to_plane(x, t, h, l) if x == h else ((x, l), 2 * x + t)


def far_both(x, t, h, l):
    return ((x, l), 2 * (1 - x) + t) if x == h else ((x, l), 2 * x + t)


def move(x, rule, name):
    with jax.named_scope(name):
        return lax.ppermute(x, GRID, route(rule))


def after(x, *others):
    return lax.optimization_barrier((x, *others))[0]


def gather_four(masked, top, low, inverse_blocks, halved, swap):
    rows, cols = masked.shape
    row, col = lax.axis_index("row"), lax.axis_index("col")
    near_side = (row // 2) == (col // 2)
    same = ((row % 2) == (col % 2)).astype(jnp.int32).reshape(1)
    half, whole = ((rows // 2, cols), F32), ((rows, cols), F32)

    low_crossed = move(low, cross_early, "low_crossed")
    top_moved = move(top, far_direct, "top_moved")
    low_next = jnp.where(near_side, low_crossed, low)
    low_moved = move(low_next, far_both, "low_moved")
    halves = halved(after(inverse_blocks, low_next))
    low_flip = swap(after(low_crossed, *halves), "row", 2, "low_flip")
    top_flip = swap(top_moved, "row", 2, "top_flip")
    near = jnp.where(
        near_side,
        jnp.concatenate([top_flip, low_flip]),
        jnp.concatenate([top_moved, low_crossed]),
    )
    far = jnp.concatenate([jnp.where(near_side, top_moved, top_flip), low_moved])
    near_other = swap(near, "row", 1, "near_cores")

    far_other = swap(far, "row", 1, "far_cores")
    outs = call(
        pair, [SMEM] + [VMEM] * 4, [half] * 4, (same, *halves, far, far_other), 12, "far_pair"
    )
    two, three = outs[:2], outs[2:]
    own, near1 = call(
        pair, [SMEM] + [VMEM] * 4, [whole] * 2, (same, *halves, near, near_other), 12, "near_pair"
    )
    near1 = swap(near1, "col", 1, "near_partial")
    sums = [a + swap(b, "col", 1, "next") for a, b in zip(two, three)]
    return [own, near1, *[swap(x, "col", 2, "across") for x in sums]]


def on_device(side, inverse_blocks, lower_panel, struct_mask, diag_inverse):
    width = diag_inverse.shape[1]
    rows, cols = lower_panel.shape

    def swap(x, axis, bit, name="swap"):
        with jax.named_scope(name):
            return lax.ppermute(x, axis, [(i, i ^ bit) for i in range(side)])

    mask = struct_mask.T
    blocks = struct_mask.shape[0]
    four = side == 4 and blocks % 2 == 0

    def masked_rows(*spans, grant=4):
        return call(
            functools.partial(masking, spans),
            [SMEM, VMEM],
            [((rows * (last - first) // blocks, cols), F32) for first, last in spans],
            (mask, lower_panel),
            grant,
            "masking",
        )

    def halved(matrix):
        return call(
            splitting,
            [VMEM],
            [(matrix.shape, jnp.bfloat16)] * 2,
            (matrix,),
            8,
            "splitting",
            20_000_000_000,
        )

    if four:
        (low,) = masked_rows((blocks // 2, blocks), grant=60)
        masked, top = masked_rows((0, blocks), (0, blocks // 2))
        arrived = gather_four(masked, top, low, inverse_blocks, halved, swap)
    else:
        (masked,) = masked_rows((0, blocks))
        arrived = gather_any(side, masked, halved(inverse_blocks), swap)

    if four:
        (quad,) = call(
            functools.partial(quad_only, width),
            [SMEM] + [VMEM] * (1 + len(arrived)),
            [((cols, width), F32)],
            (mask, masked, *arrived),
            16,
            "quad",
            scratch=[pltpu.VMEM((rows, cols), F32)],
        )
        late = lax.optimization_barrier((quad, *arrived))[1:]
        (g_panel,) = call(
            functools.partial(panel_only, width),
            [SMEM] + [VMEM] * len(arrived),
            [((rows, cols), F32)],
            (mask, *late),
            16,
            "panel",
        )
    else:
        g_panel, quad = call(
            functools.partial(finish, width),
            [SMEM] + [VMEM] * (1 + len(arrived)),
            [((rows, cols), F32), ((cols, width), F32)],
            (mask, masked, *arrived),
            16,
            "finish",
        )
    if four:
        for part in [swap(quad, "row", bit, "tail") for bit in range(1, side)]:
            quad = quad + part
        return g_panel, diag_inverse + quad
    bit = 1
    while bit < side:
        quad = quad + swap(quad, "row", bit)
        bit *= 2
    return g_panel, diag_inverse + quad


def solution(mesh):
    side = mesh.shape["row"]
    assert side == mesh.shape["col"] and side & (side - 1) == 0
    placed = (
        P(("pole", "row"), "col"),
        P(("pole", "row"), "col"),
        P("row", "col"),
        P(("pole", "col"), None),
    )
    return jax.shard_map(
        functools.partial(on_device, side),
        mesh=mesh,
        in_specs=placed,
        out_specs=(P(("pole", "row"), "col"), P(("pole", "col"), None)),
        check_vma=False,
    )
```

```python
import functools

import jax
import jax.numpy as jnp
from jax import lax
from jax.experimental import pallas as pl
from jax.experimental.pallas import tpu as pltpu
from jax.sharding import PartitionSpec as P

GRID = ("row", "col")
VMEM = pl.BlockSpec(memory_space=pltpu.VMEM)
SMEM = pl.BlockSpec(memory_space=pltpu.SMEM)
F32 = jnp.float32
ROWS = ((0,), (0,))
INNER = ((1,), (0,))


def split(x):
    high = x.astype(jnp.bfloat16)
    return high, (x - high.astype(F32)).astype(jnp.bfloat16)


def dot(a, b, dims):
    return lax.dot_general(a, b, (dims, ((), ())), preferred_element_type=F32)


def call(body, ins, outs, args, grant, name, flops=None, scratch=()):
    return pl.pallas_call(
        body,
        out_shape=[jax.ShapeDtypeStruct(shape, dtype) for shape, dtype in outs],
        in_specs=ins,
        out_specs=[VMEM] * len(outs),
        scratch_shapes=scratch,
        compiler_params=pltpu.CompilerParams(vmem_limit_bytes=grant << 20),
        cost_estimate=flops
        and pl.CostEstimate(flops=flops, bytes_accessed=0, transcendentals=0),
        name=name,
    )(*args)


def masking(spans, mask_ref, panel_ref, *out_refs):
    supers, blocks = mask_ref.shape
    tall, wide = panel_ref.shape[0] // blocks, panel_ref.shape[1] // supers
    for (first, last), ref in zip(spans, out_refs):
        for b in range(first, last):
            for s in range(supers):
                cols = slice(s * wide, (s + 1) * wide)
                block = panel_ref[b * tall : (b + 1) * tall, cols]
                at = (b - first) * tall
                ref[at : at + tall, cols] = block * mask_ref[s, b].astype(F32)


def splitting(a_ref, high_ref, low_ref):
    high_ref[...], low_ref[...] = split(a_ref[...])


def product(ah, al, m):
    mh, ml = split(m)
    width = m.shape[1]
    first = dot(ah, jnp.concatenate([mh, ml], axis=1), INNER)
    return first[:, :width] + (first[:, width:] + dot(al, mh, INNER))


def products(count, shift_ref, high_ref, low_ref, *refs):
    panels, outs = refs[:count], refs[count:]
    ah, al = high_ref[...], low_ref[...]
    shift = shift_ref[0]
    for i in range(count):
        m = panels[0][...]
        for j in range(1, count):
            m = jnp.where(shift == (i ^ j), panels[j][...], m)
        outs[i][...] = product(ah, al, m)


def pair(same_ref, high_ref, low_ref, mine_ref, other_ref, *outs):
    ah, al = high_ref[...], low_ref[...]
    same = same_ref[0] == 1
    mine, other = mine_ref[...], other_ref[...]
    for m, refs in (
        (jnp.where(same, mine, other), outs[: len(outs) // 2]),
        (jnp.where(same, other, mine), outs[len(outs) // 2 :]),
    ):
        out = product(ah, al, m)
        tall = out.shape[0] // len(refs)
        for i, ref in enumerate(refs):
            ref[...] = out[i * tall : (i + 1) * tall, :]


def finish(width, mask_ref, masked_ref, *refs):
    parts, g_ref, quad_ref = refs[:-2], refs[-2], refs[-1]
    rows = g_ref.shape[0]
    supers, blocks = mask_ref.shape
    tall = rows // blocks
    for b in range(blocks):
        for s in range(supers):
            cols = slice(s * width, (s + 1) * width)
            total = None
            for whole in parts:
                pieces = whole if isinstance(whole, tuple) else (whole,)
                depth = rows // len(pieces)
                ref, at = pieces[b * tall // depth], b * tall % depth
                term = ref[at : at + tall, cols]
                total = term if total is None else total + term
            g_ref[b * tall : (b + 1) * tall, cols] = total * -mask_ref[s, b].astype(F32)
    for s in range(supers if quad_ref is not None else 0):
        cols = slice(s * width, (s + 1) * width)
        mh, ml = split(masked_ref[:, cols])
        gh, gl = split(g_ref[:, cols])
        quad_ref[cols, :] = -(dot(mh, gh, ROWS) + (dot(mh, gl, ROWS) + dot(ml, gh, ROWS)))


def quad_only(width, mask_ref, masked_ref, own, near, *refs):
    *fars, g_ref, quad_ref = refs[:-2] + (refs[-1], refs[-2])
    finish(width, mask_ref, masked_ref, own, near, tuple(fars), g_ref, quad_ref)


def panel_only(width, mask_ref, own, near, *refs):
    finish(width, mask_ref, None, own, near, tuple(refs[:-1]), refs[-1], None)


def gather_any(side, masked, halves, swap):
    rows, cols = masked.shape
    turned = lax.ppermute(
        masked, GRID, [(r * side + c, c * side + r) for r in range(side) for c in range(side)]
    )
    turned, *halves = lax.optimization_barrier((turned, *halves))
    panels = {0: turned}
    bit = side // 2
    while bit:
        for j, x in list(panels.items()):
            panels[j ^ bit] = swap(x, "row", bit)
        bit //= 2
    shift = jnp.bitwise_xor(lax.axis_index("row"), lax.axis_index("col"))
    partials = call(
        functools.partial(products, side),
        [SMEM] + [VMEM] * (2 + side),
        [((rows, cols), F32)] * side,
        (shift.astype(jnp.int32).reshape(1), *halves, *[panels[j] for j in range(side)]),
        48,
        "products",
    )
    return [partials[0]] + [swap(partials[i], "col", i) for i in range(1, side)]


def route(rule):
    pairs = []
    for x in range(2):
        for t in range(2):
            for h in range(2):
                for l in range(2):
                    to = rule(x, t, h, l)
                    if to is not None:
                        (x2, t2), z2 = to
                        pairs.append((8 * x + 4 * t + 2 * h + l, 8 * x2 + 4 * t2 + z2))
    return pairs


def to_plane(x, t, h, l):
    return ((1 - h, t), 2 * h + l) if t == l else ((1 - h, 1 - t), 2 * h + t)


def cross_early(x, t, h, l):
    return to_plane(x, t, h, l) if x == h else ((1 - x, t), 2 * h + l)


def far_direct(x, t, h, l):
    return to_plane(x, t, h, l) if x == h else ((x, l), 2 * x + t)


def far_both(x, t, h, l):
    return ((x, l), 2 * (1 - x) + t) if x == h else ((x, l), 2 * x + t)


def move(x, rule, name):
    with jax.named_scope(name):
        return lax.ppermute(x, GRID, route(rule))


def after(x, *others):
    return lax.optimization_barrier((x, *others))[0]


def gather_four(masked, top, low, inverse_blocks, halved, swap):
    rows, cols = masked.shape
    row, col = lax.axis_index("row"), lax.axis_index("col")
    near_side = (row // 2) == (col // 2)
    same = ((row % 2) == (col % 2)).astype(jnp.int32).reshape(1)
    half, whole = ((rows // 2, cols), F32), ((rows, cols), F32)

    low_crossed = move(low, cross_early, "low_crossed")
    top_moved = move(top, far_direct, "top_moved")
    halves = halved(after(inverse_blocks, top))
    low_next = jnp.where(near_side, after(low_crossed, *halves), low)
    low_moved = move(low_next, far_both, "low_moved")
    top_flip = swap(top_moved, "row", 2, "top_flip")
    low_flip = swap(after(low_crossed, low_moved), "row", 2, "low_flip")
    near = jnp.where(
        near_side,
        jnp.concatenate([top_flip, low_flip]),
        jnp.concatenate([top_moved, low_crossed]),
    )
    far = jnp.concatenate([jnp.where(near_side, top_moved, top_flip), low_moved])
    near_other = swap(near, "row", 1, "near_cores")

    far_other = swap(far, "row", 1, "far_cores")
    outs = call(
        pair, [SMEM] + [VMEM] * 4, [half] * 4, (same, *halves, far, far_other), 12, "far_pair"
    )
    two, three = outs[:2], outs[2:]
    own, near1 = call(
        pair, [SMEM] + [VMEM] * 4, [whole] * 2, (same, *halves, near, near_other), 12, "near_pair"
    )
    near1 = swap(near1, "col", 1, "near_partial")
    sums = [a + swap(b, "col", 1, "next") for a, b in zip(two, three)]
    return [own, near1, *[swap(x, "col", 2, "across") for x in sums]]


def on_device(side, inverse_blocks, lower_panel, struct_mask, diag_inverse):
    width = diag_inverse.shape[1]
    rows, cols = lower_panel.shape

    def swap(x, axis, bit, name="swap"):
        with jax.named_scope(name):
            return lax.ppermute(x, axis, [(i, i ^ bit) for i in range(side)])

    mask = struct_mask.T
    blocks = struct_mask.shape[0]
    four = side == 4 and blocks % 2 == 0

    def masked_rows(*spans, grant=4):
        return call(
            functools.partial(masking, spans),
            [SMEM, VMEM],
            [((rows * (last - first) // blocks, cols), F32) for first, last in spans],
            (mask, lower_panel),
            grant,
            "masking",
        )

    def halved(matrix):
        return call(
            splitting,
            [VMEM],
            [(matrix.shape, jnp.bfloat16)] * 2,
            (matrix,),
            8,
            "splitting",
            20_000_000_000,
        )

    if four:
        (low,) = masked_rows((blocks // 2, blocks), grant=60)
        masked, top = masked_rows((0, blocks), (0, blocks // 2))
        arrived = gather_four(masked, top, low, inverse_blocks, halved, swap)
    else:
        (masked,) = masked_rows((0, blocks))
        arrived = gather_any(side, masked, halved(inverse_blocks), swap)

    if four:
        (quad,) = call(
            functools.partial(quad_only, width),
            [SMEM] + [VMEM] * (1 + len(arrived)),
            [((cols, width), F32)],
            (mask, masked, *arrived),
            16,
            "quad",
            scratch=[pltpu.VMEM((rows, cols), F32)],
        )
        late = lax.optimization_barrier((quad, *arrived))[1:]
        (g_panel,) = call(
            functools.partial(panel_only, width),
            [SMEM] + [VMEM] * len(arrived),
            [((rows, cols), F32)],
            (mask, *late),
            16,
            "panel",
        )
    else:
        g_panel, quad = call(
            functools.partial(finish, width),
            [SMEM] + [VMEM] * (1 + len(arrived)),
            [((rows, cols), F32), ((cols, width), F32)],
            (mask, masked, *arrived),
            16,
            "finish",
        )
    if four:
        for part in [swap(quad, "row", bit, "tail") for bit in range(1, side)]:
            quad = quad + part
        return g_panel, diag_inverse + quad
    bit = 1
    while bit < side:
        quad = quad + swap(quad, "row", bit)
        bit *= 2
    return g_panel, diag_inverse + quad


def solution(mesh):
    side = mesh.shape["row"]
    assert side == mesh.shape["col"] and side & (side - 1) == 0
    placed = (
        P(("pole", "row"), "col"),
        P(("pole", "row"), "col"),
        P("row", "col"),
        P(("pole", "col"), None),
    )
    return jax.shard_map(
        functools.partial(on_device, side),
        mesh=mesh,
        in_specs=placed,
        out_specs=(P(("pole", "row"), "col"), P(("pole", "col"), None)),
        check_vma=False,
    )
```

```python
import functools

import jax
import jax.numpy as jnp
from jax import lax
from jax.experimental import pallas as pl
from jax.experimental.pallas import tpu as pltpu
from jax.sharding import PartitionSpec as P

GRID = ("row", "col")
VMEM = pl.BlockSpec(memory_space=pltpu.VMEM)
SMEM = pl.BlockSpec(memory_space=pltpu.SMEM)
F32 = jnp.float32
ROWS = ((0,), (0,))
INNER = ((1,), (0,))


def split(x):
    high = x.astype(jnp.bfloat16)
    return high, (x - high.astype(F32)).astype(jnp.bfloat16)


def dot(a, b, dims):
    return lax.dot_general(a, b, (dims, ((), ())), preferred_element_type=F32)


def call(body, ins, outs, args, grant, name, flops=None, scratch=()):
    return pl.pallas_call(
        body,
        out_shape=[jax.ShapeDtypeStruct(shape, dtype) for shape, dtype in outs],
        in_specs=ins,
        out_specs=[VMEM] * len(outs),
        scratch_shapes=scratch,
        compiler_params=pltpu.CompilerParams(vmem_limit_bytes=grant << 20),
        cost_estimate=flops
        and pl.CostEstimate(flops=flops, bytes_accessed=0, transcendentals=0),
        name=name,
    )(*args)


def masking(spans, mask_ref, panel_ref, *out_refs):
    supers, blocks = mask_ref.shape
    tall, wide = panel_ref.shape[0] // blocks, panel_ref.shape[1] // supers
    for (first, last), ref in zip(spans, out_refs):
        for b in range(first, last):
            for s in range(supers):
                cols = slice(s * wide, (s + 1) * wide)
                block = panel_ref[b * tall : (b + 1) * tall, cols]
                at = (b - first) * tall
                ref[at : at + tall, cols] = block * mask_ref[s, b].astype(F32)


def splitting(a_ref, high_ref, low_ref):
    high_ref[...], low_ref[...] = split(a_ref[...])


def product(ah, al, m):
    mh, ml = split(m)
    width = m.shape[1]
    first = dot(ah, jnp.concatenate([mh, ml], axis=1), INNER)
    return first[:, :width] + (first[:, width:] + dot(al, mh, INNER))


def products(count, shift_ref, high_ref, low_ref, *refs):
    panels, outs = refs[:count], refs[count:]
    ah, al = high_ref[...], low_ref[...]
    shift = shift_ref[0]
    for i in range(count):
        m = panels[0][...]
        for j in range(1, count):
            m = jnp.where(shift == (i ^ j), panels[j][...], m)
        outs[i][...] = product(ah, al, m)


def pair(same_ref, high_ref, low_ref, mine_ref, other_ref, *outs):
    same = same_ref[0] == 1
    mine, other = mine_ref[...], other_ref[...]
    width = mine.shape[1]
    first, second = jnp.where(same, mine, other), jnp.where(same, other, mine)
    (h0, l0), (h1, l1) = split(first), split(second)
    ah = high_ref[...]
    low = dot(low_ref[...], jnp.concatenate([h0, h1], axis=1), INNER)
    n = len(outs) // 2
    for i, (h, l) in enumerate(((h0, l0), (h1, l1))):
        both = dot(ah, jnp.concatenate([h, l], axis=1), INNER)
        out = both[:, :width] + (both[:, width:] + low[:, i * width : (i + 1) * width])
        tall = out.shape[0] // n
        for j, ref in enumerate(outs[i * n : (i + 1) * n]):
            ref[...] = out[j * tall : (j + 1) * tall, :]


def finish(width, mask_ref, masked_ref, *refs):
    parts, g_ref, quad_ref = refs[:-2], refs[-2], refs[-1]
    rows = g_ref.shape[0]
    supers, blocks = mask_ref.shape
    tall = rows // blocks
    for b in range(blocks):
        for s in range(supers):
            cols = slice(s * width, (s + 1) * width)
            total = None
            for whole in parts:
                pieces = whole if isinstance(whole, tuple) else (whole,)
                depth = rows // len(pieces)
                ref, at = pieces[b * tall // depth], b * tall % depth
                term = ref[at : at + tall, cols]
                total = term if total is None else total + term
            g_ref[b * tall : (b + 1) * tall, cols] = total * -mask_ref[s, b].astype(F32)
    for s in range(supers if quad_ref is not None else 0):
        cols = slice(s * width, (s + 1) * width)
        mh, ml = split(masked_ref[:, cols])
        gh, gl = split(g_ref[:, cols])
        quad_ref[cols, :] = -(dot(mh, gh, ROWS) + (dot(mh, gl, ROWS) + dot(ml, gh, ROWS)))


def quad_only(width, mask_ref, masked_ref, own, near, *refs):
    *fars, g_ref, quad_ref = refs[:-2] + (refs[-1], refs[-2])
    finish(width, mask_ref, masked_ref, own, near, tuple(fars), g_ref, quad_ref)


def panel_only(width, mask_ref, own, near, *refs):
    finish(width, mask_ref, None, own, near, tuple(refs[:-1]), refs[-1], None)


def gather_any(side, masked, halves, swap):
    rows, cols = masked.shape
    turned = lax.ppermute(
        masked, GRID, [(r * side + c, c * side + r) for r in range(side) for c in range(side)]
    )
    turned, *halves = lax.optimization_barrier((turned, *halves))
    panels = {0: turned}
    bit = side // 2
    while bit:
        for j, x in list(panels.items()):
            panels[j ^ bit] = swap(x, "row", bit)
        bit //= 2
    shift = jnp.bitwise_xor(lax.axis_index("row"), lax.axis_index("col"))
    partials = call(
        functools.partial(products, side),
        [SMEM] + [VMEM] * (2 + side),
        [((rows, cols), F32)] * side,
        (shift.astype(jnp.int32).reshape(1), *halves, *[panels[j] for j in range(side)]),
        48,
        "products",
    )
    return [partials[0]] + [swap(partials[i], "col", i) for i in range(1, side)]


def route(rule):
    pairs = []
    for x in range(2):
        for t in range(2):
            for h in range(2):
                for l in range(2):
                    to = rule(x, t, h, l)
                    if to is not None:
                        (x2, t2), z2 = to
                        pairs.append((8 * x + 4 * t + 2 * h + l, 8 * x2 + 4 * t2 + z2))
    return pairs


def to_plane(x, t, h, l):
    return ((1 - h, t), 2 * h + l) if t == l else ((1 - h, 1 - t), 2 * h + t)


def cross_early(x, t, h, l):
    return to_plane(x, t, h, l) if x == h else ((1 - x, t), 2 * h + l)


def far_direct(x, t, h, l):
    return to_plane(x, t, h, l) if x == h else ((x, l), 2 * x + t)


def far_both(x, t, h, l):
    return ((x, l), 2 * (1 - x) + t) if x == h else ((x, l), 2 * x + t)


def move(x, rule, name):
    with jax.named_scope(name):
        return lax.ppermute(x, GRID, route(rule))


def after(x, *others):
    return lax.optimization_barrier((x, *others))[0]


def gather_four(masked, top, low, inverse_blocks, halved, swap):
    rows, cols = masked.shape
    row, col = lax.axis_index("row"), lax.axis_index("col")
    near_side = (row // 2) == (col // 2)
    same = ((row % 2) == (col % 2)).astype(jnp.int32).reshape(1)
    half, whole = ((rows // 2, cols), F32), ((rows, cols), F32)

    low_crossed = move(low, cross_early, "low_crossed")
    top_moved = move(top, far_direct, "top_moved")
    halves = halved(after(inverse_blocks, top))
    low_next = jnp.where(near_side, after(low_crossed, *halves), low)
    low_moved = move(low_next, far_both, "low_moved")
    top_flip = swap(top_moved, "row", 2, "top_flip")
    low_flip = swap(after(low_crossed, low_moved), "row", 2, "low_flip")
    near = jnp.where(
        near_side,
        jnp.concatenate([top_flip, low_flip]),
        jnp.concatenate([top_moved, low_crossed]),
    )
    far = jnp.concatenate([jnp.where(near_side, top_moved, top_flip), low_moved])
    near_other = swap(near, "row", 1, "near_cores")

    far_other = swap(far, "row", 1, "far_cores")
    outs = call(
        pair, [SMEM] + [VMEM] * 4, [half] * 4, (same, *halves, far, far_other), 12, "far_pair"
    )
    two, three = outs[:2], outs[2:]
    own, near1 = call(
        pair, [SMEM] + [VMEM] * 4, [whole] * 2, (same, *halves, near, near_other), 12, "near_pair"
    )
    near1 = swap(near1, "col", 1, "near_partial")
    sums = [a + swap(b, "col", 1, "next") for a, b in zip(two, three)]
    return [own, near1, *[swap(x, "col", 2, "across") for x in sums]]


def on_device(side, inverse_blocks, lower_panel, struct_mask, diag_inverse):
    width = diag_inverse.shape[1]
    rows, cols = lower_panel.shape

    def swap(x, axis, bit, name="swap"):
        with jax.named_scope(name):
            return lax.ppermute(x, axis, [(i, i ^ bit) for i in range(side)])

    mask = struct_mask.T
    blocks = struct_mask.shape[0]
    four = side == 4 and blocks % 2 == 0

    def masked_rows(*spans, grant=4):
        return call(
            functools.partial(masking, spans),
            [SMEM, VMEM],
            [((rows * (last - first) // blocks, cols), F32) for first, last in spans],
            (mask, lower_panel),
            grant,
            "masking",
        )

    def halved(matrix):
        return call(
            splitting,
            [VMEM],
            [(matrix.shape, jnp.bfloat16)] * 2,
            (matrix,),
            8,
            "splitting",
            20_000_000_000,
        )

    if four:
        (low,) = masked_rows((blocks // 2, blocks), grant=60)
        masked, top = masked_rows((0, blocks), (0, blocks // 2))
        arrived = gather_four(masked, top, low, inverse_blocks, halved, swap)
    else:
        (masked,) = masked_rows((0, blocks))
        arrived = gather_any(side, masked, halved(inverse_blocks), swap)

    if four:
        (quad,) = call(
            functools.partial(quad_only, width),
            [SMEM] + [VMEM] * (1 + len(arrived)),
            [((cols, width), F32)],
            (mask, masked, *arrived),
            16,
            "quad",
            scratch=[pltpu.VMEM((rows, cols), F32)],
        )
        late = lax.optimization_barrier((quad, *arrived))[1:]
        (g_panel,) = call(
            functools.partial(panel_only, width),
            [SMEM] + [VMEM] * len(arrived),
            [((rows, cols), F32)],
            (mask, *late),
            16,
            "panel",
        )
    else:
        g_panel, quad = call(
            functools.partial(finish, width),
            [SMEM] + [VMEM] * (1 + len(arrived)),
            [((rows, cols), F32), ((cols, width), F32)],
            (mask, masked, *arrived),
            16,
            "finish",
        )
    if four:
        for part in [swap(quad, "row", bit, "tail") for bit in range(1, side)]:
            quad = quad + part
        return g_panel, diag_inverse + quad
    bit = 1
    while bit < side:
        quad = quad + swap(quad, "row", bit)
        bit *= 2
    return g_panel, diag_inverse + quad


def solution(mesh):
    side = mesh.shape["row"]
    assert side == mesh.shape["col"] and side & (side - 1) == 0
    placed = (
        P(("pole", "row"), "col"),
        P(("pole", "row"), "col"),
        P("row", "col"),
        P(("pole", "col"), None),
    )
    return jax.shard_map(
        functools.partial(on_device, side),
        mesh=mesh,
        in_specs=placed,
        out_specs=(P(("pole", "row"), "col"), P(("pole", "col"), None)),
        check_vma=False,
    )
```

```python
import functools

import jax
import jax.numpy as jnp
from jax import lax
from jax.experimental import pallas as pl
from jax.experimental.pallas import tpu as pltpu
from jax.sharding import PartitionSpec as P

GRID = ("row", "col")
VMEM = pl.BlockSpec(memory_space=pltpu.VMEM)
SMEM = pl.BlockSpec(memory_space=pltpu.SMEM)
F32 = jnp.float32
ROWS = ((0,), (0,))
INNER = ((1,), (0,))


def split(x):
    high = x.astype(jnp.bfloat16)
    return high, (x - high.astype(F32)).astype(jnp.bfloat16)


def dot(a, b, dims):
    return lax.dot_general(a, b, (dims, ((), ())), preferred_element_type=F32)


def call(body, ins, outs, args, grant, name, flops=None, scratch=()):
    return pl.pallas_call(
        body,
        out_shape=[jax.ShapeDtypeStruct(shape, dtype) for shape, dtype in outs],
        in_specs=ins,
        out_specs=[VMEM] * len(outs),
        scratch_shapes=scratch,
        compiler_params=pltpu.CompilerParams(vmem_limit_bytes=grant << 20),
        cost_estimate=flops
        and pl.CostEstimate(flops=flops, bytes_accessed=0, transcendentals=0),
        name=name,
    )(*args)


def masking(spans, mask_ref, panel_ref, *out_refs):
    supers, blocks = mask_ref.shape
    tall, wide = panel_ref.shape[0] // blocks, panel_ref.shape[1] // supers
    for (first, last), ref in zip(spans, out_refs):
        for b in range(first, last):
            for s in range(supers):
                cols = slice(s * wide, (s + 1) * wide)
                block = panel_ref[b * tall : (b + 1) * tall, cols]
                at = (b - first) * tall
                ref[at : at + tall, cols] = block * mask_ref[s, b].astype(F32)


def splitting(a_ref, high_ref, low_ref):
    high_ref[...], low_ref[...] = split(a_ref[...])


def product(ah, al, m):
    mh, ml = split(m)
    width = m.shape[1]
    first = dot(ah, jnp.concatenate([mh, ml], axis=1), INNER)
    return first[:, :width] + (first[:, width:] + dot(al, mh, INNER))


def products(count, shift_ref, high_ref, low_ref, *refs):
    panels, outs = refs[:count], refs[count:]
    ah, al = high_ref[...], low_ref[...]
    shift = shift_ref[0]
    for i in range(count):
        m = panels[0][...]
        for j in range(1, count):
            m = jnp.where(shift == (i ^ j), panels[j][...], m)
        outs[i][...] = product(ah, al, m)


def pair(same_ref, high_ref, low_ref, mine_ref, other_ref, *outs):
    same = same_ref[0] == 1
    mine, other = mine_ref[...], other_ref[...]
    width = mine.shape[1]
    first, second = jnp.where(same, mine, other), jnp.where(same, other, mine)
    (h0, l0), (h1, l1) = split(first), split(second)
    ah = high_ref[...]
    low = dot(low_ref[...], jnp.concatenate([h0, h1], axis=1), INNER)
    n = len(outs) // 2
    for i, (h, l) in enumerate(((h0, l0), (h1, l1))):
        both = dot(ah, jnp.concatenate([h, l], axis=1), INNER)
        out = both[:, :width] + (both[:, width:] + low[:, i * width : (i + 1) * width])
        tall = out.shape[0] // n
        for j, ref in enumerate(outs[i * n : (i + 1) * n]):
            ref[...] = out[j * tall : (j + 1) * tall, :]


def finish(width, mask_ref, masked_ref, *refs):
    parts, g_ref, quad_ref = refs[:-2], refs[-2], refs[-1]
    rows = g_ref.shape[0]
    supers, blocks = mask_ref.shape
    tall = rows // blocks
    for b in range(blocks):
        for s in range(supers):
            cols = slice(s * width, (s + 1) * width)
            total = None
            for whole in parts:
                pieces = whole if isinstance(whole, tuple) else (whole,)
                depth = rows // len(pieces)
                ref, at = pieces[b * tall // depth], b * tall % depth
                term = ref[at : at + tall, cols]
                total = term if total is None else total + term
            g_ref[b * tall : (b + 1) * tall, cols] = total * -mask_ref[s, b].astype(F32)
    for s in range(supers if quad_ref is not None else 0):
        cols = slice(s * width, (s + 1) * width)
        mh, ml = split(masked_ref[:, cols])
        gh, gl = split(g_ref[:, cols])
        both = dot(mh, jnp.concatenate([gh, gl], axis=1), ROWS)
        quad_ref[cols, :] = -(both[:, :width] + (both[:, width:] + dot(ml, gh, ROWS)))


def quad_only(width, mask_ref, masked_ref, own, near, *refs):
    *fars, g_ref, quad_ref = refs[:-2] + (refs[-1], refs[-2])
    finish(width, mask_ref, masked_ref, own, near, tuple(fars), g_ref, quad_ref)


def panel_only(width, mask_ref, own, near, *refs):
    finish(width, mask_ref, None, own, near, tuple(refs[:-1]), refs[-1], None)


def gather_any(side, masked, halves, swap):
    rows, cols = masked.shape
    turned = lax.ppermute(
        masked, GRID, [(r * side + c, c * side + r) for r in range(side) for c in range(side)]
    )
    turned, *halves = lax.optimization_barrier((turned, *halves))
    panels = {0: turned}
    bit = side // 2
    while bit:
        for j, x in list(panels.items()):
            panels[j ^ bit] = swap(x, "row", bit)
        bit //= 2
    shift = jnp.bitwise_xor(lax.axis_index("row"), lax.axis_index("col"))
    partials = call(
        functools.partial(products, side),
        [SMEM] + [VMEM] * (2 + side),
        [((rows, cols), F32)] * side,
        (shift.astype(jnp.int32).reshape(1), *halves, *[panels[j] for j in range(side)]),
        48,
        "products",
    )
    return [partials[0]] + [swap(partials[i], "col", i) for i in range(1, side)]


def route(rule):
    pairs = []
    for x in range(2):
        for t in range(2):
            for h in range(2):
                for l in range(2):
                    to = rule(x, t, h, l)
                    if to is not None:
                        (x2, t2), z2 = to
                        pairs.append((8 * x + 4 * t + 2 * h + l, 8 * x2 + 4 * t2 + z2))
    return pairs


def to_plane(x, t, h, l):
    return ((1 - h, t), 2 * h + l) if t == l else ((1 - h, 1 - t), 2 * h + t)


def cross_early(x, t, h, l):
    return to_plane(x, t, h, l) if x == h else ((1 - x, t), 2 * h + l)


def far_direct(x, t, h, l):
    return to_plane(x, t, h, l) if x == h else ((x, l), 2 * x + t)


def far_both(x, t, h, l):
    return ((x, l), 2 * (1 - x) + t) if x == h else ((x, l), 2 * x + t)


def move(x, rule, name):
    with jax.named_scope(name):
        return lax.ppermute(x, GRID, route(rule))


def after(x, *others):
    return lax.optimization_barrier((x, *others))[0]


def gather_four(masked, top, low, inverse_blocks, halved, swap):
    rows, cols = masked.shape
    row, col = lax.axis_index("row"), lax.axis_index("col")
    near_side = (row // 2) == (col // 2)
    same = ((row % 2) == (col % 2)).astype(jnp.int32).reshape(1)
    half, whole = ((rows // 2, cols), F32), ((rows, cols), F32)

    low_crossed = move(low, cross_early, "low_crossed")
    top_moved = move(top, far_direct, "top_moved")
    halves = halved(after(inverse_blocks, top))
    low_next = jnp.where(near_side, after(low_crossed, *halves), low)
    low_moved = move(low_next, far_both, "low_moved")
    top_flip = swap(top_moved, "row", 2, "top_flip")
    low_flip = swap(after(low_crossed, low_moved), "row", 2, "low_flip")
    near = jnp.where(
        near_side,
        jnp.concatenate([top_flip, low_flip]),
        jnp.concatenate([top_moved, low_crossed]),
    )
    far = jnp.concatenate([jnp.where(near_side, top_moved, top_flip), low_moved])
    near_other = swap(near, "row", 1, "near_cores")

    far_other = swap(far, "row", 1, "far_cores")
    outs = call(
        pair, [SMEM] + [VMEM] * 4, [half] * 4, (same, *halves, far, far_other), 12, "far_pair"
    )
    two, three = outs[:2], outs[2:]
    own, near1 = call(
        pair, [SMEM] + [VMEM] * 4, [whole] * 2, (same, *halves, near, near_other), 12, "near_pair"
    )
    near1 = swap(near1, "col", 1, "near_partial")
    sums = [a + swap(b, "col", 1, "next") for a, b in zip(two, three)]
    return [own, near1, *[swap(x, "col", 2, "across") for x in sums]]


def on_device(side, inverse_blocks, lower_panel, struct_mask, diag_inverse):
    width = diag_inverse.shape[1]
    rows, cols = lower_panel.shape

    def swap(x, axis, bit, name="swap"):
        with jax.named_scope(name):
            return lax.ppermute(x, axis, [(i, i ^ bit) for i in range(side)])

    mask = struct_mask.T
    blocks = struct_mask.shape[0]
    four = side == 4 and blocks % 2 == 0

    def masked_rows(*spans, grant=4):
        return call(
            functools.partial(masking, spans),
            [SMEM, VMEM],
            [((rows * (last - first) // blocks, cols), F32) for first, last in spans],
            (mask, lower_panel),
            grant,
            "masking",
        )

    def halved(matrix):
        return call(
            splitting,
            [VMEM],
            [(matrix.shape, jnp.bfloat16)] * 2,
            (matrix,),
            8,
            "splitting",
            20_000_000_000,
        )

    if four:
        (low,) = masked_rows((blocks // 2, blocks), grant=60)
        masked, top = masked_rows((0, blocks), (0, blocks // 2))
        arrived = gather_four(masked, top, low, inverse_blocks, halved, swap)
    else:
        (masked,) = masked_rows((0, blocks))
        arrived = gather_any(side, masked, halved(inverse_blocks), swap)

    if four:
        (quad,) = call(
            functools.partial(quad_only, width),
            [SMEM] + [VMEM] * (1 + len(arrived)),
            [((cols, width), F32)],
            (mask, masked, *arrived),
            16,
            "quad",
            scratch=[pltpu.VMEM((rows, cols), F32)],
        )
        late = lax.optimization_barrier((quad, *arrived))[1:]
        (g_panel,) = call(
            functools.partial(panel_only, width),
            [SMEM] + [VMEM] * len(arrived),
            [((rows, cols), F32)],
            (mask, *late),
            16,
            "panel",
        )
    else:
        g_panel, quad = call(
            functools.partial(finish, width),
            [SMEM] + [VMEM] * (1 + len(arrived)),
            [((rows, cols), F32), ((cols, width), F32)],
            (mask, masked, *arrived),
            16,
            "finish",
        )
    if four:
        for part in [swap(quad, "row", bit, "tail") for bit in range(1, side)]:
            quad = quad + part
        return g_panel, diag_inverse + quad
    bit = 1
    while bit < side:
        quad = quad + swap(quad, "row", bit)
        bit *= 2
    return g_panel, diag_inverse + quad


def solution(mesh):
    side = mesh.shape["row"]
    assert side == mesh.shape["col"] and side & (side - 1) == 0
    placed = (
        P(("pole", "row"), "col"),
        P(("pole", "row"), "col"),
        P("row", "col"),
        P(("pole", "col"), None),
    )
    return jax.shard_map(
        functools.partial(on_device, side),
        mesh=mesh,
        in_specs=placed,
        out_specs=(P(("pole", "row"), "col"), P(("pole", "col"), None)),
        check_vma=False,
    )
```

```python
import functools

import jax
import jax.numpy as jnp
from jax import lax
from jax.experimental import pallas as pl
from jax.experimental.pallas import tpu as pltpu
from jax.sharding import PartitionSpec as P

GRID = ("row", "col")
VMEM = pl.BlockSpec(memory_space=pltpu.VMEM)
SMEM = pl.BlockSpec(memory_space=pltpu.SMEM)
F32 = jnp.float32
ROWS = ((0,), (0,))
INNER = ((1,), (0,))


def split(x):
    high = x.astype(jnp.bfloat16)
    return high, (x - high.astype(F32)).astype(jnp.bfloat16)


def dot(a, b, dims):
    return lax.dot_general(a, b, (dims, ((), ())), preferred_element_type=F32)


def call(body, ins, outs, args, grant, name, flops=None, scratch=()):
    return pl.pallas_call(
        body,
        out_shape=[jax.ShapeDtypeStruct(shape, dtype) for shape, dtype in outs],
        in_specs=ins,
        out_specs=[VMEM] * len(outs),
        scratch_shapes=scratch,
        compiler_params=pltpu.CompilerParams(vmem_limit_bytes=grant << 20),
        cost_estimate=flops
        and pl.CostEstimate(flops=flops, bytes_accessed=0, transcendentals=0),
        name=name,
    )(*args)


def masking(spans, mask_ref, panel_ref, *out_refs):
    supers, blocks = mask_ref.shape
    tall, wide = panel_ref.shape[0] // blocks, panel_ref.shape[1] // supers
    for (first, last), ref in zip(spans, out_refs):
        for b in range(first, last):
            for s in range(supers):
                cols = slice(s * wide, (s + 1) * wide)
                block = panel_ref[b * tall : (b + 1) * tall, cols]
                at = (b - first) * tall
                ref[at : at + tall, cols] = block * mask_ref[s, b].astype(F32)


def splitting(a_ref, high_ref, low_ref):
    high_ref[...], low_ref[...] = split(a_ref[...])


def product(ah, al, m):
    mh, ml = split(m)
    width = m.shape[1]
    first = dot(ah, jnp.concatenate([mh, ml], axis=1), INNER)
    return first[:, :width] + (first[:, width:] + dot(al, mh, INNER))


def products(count, shift_ref, high_ref, low_ref, *refs):
    panels, outs = refs[:count], refs[count:]
    ah, al = high_ref[...], low_ref[...]
    shift = shift_ref[0]
    for i in range(count):
        m = panels[0][...]
        for j in range(1, count):
            m = jnp.where(shift == (i ^ j), panels[j][...], m)
        outs[i][...] = product(ah, al, m)


def pair(same_ref, high_ref, low_ref, mine_ref, other_ref, *outs):
    same = same_ref[0] == 1
    mine, other = mine_ref[...], other_ref[...]
    width = mine.shape[1]
    first, second = jnp.where(same, mine, other), jnp.where(same, other, mine)
    (h0, l0), (h1, l1) = split(first), split(second)
    ah = high_ref[...]
    low = dot(low_ref[...], jnp.concatenate([h0, h1], axis=1), INNER)
    n = len(outs) // 2
    for i, (h, l) in enumerate(((h0, l0), (h1, l1))):
        both = dot(ah, jnp.concatenate([h, l], axis=1), INNER)
        out = both[:, :width] + (both[:, width:] + low[:, i * width : (i + 1) * width])
        tall = out.shape[0] // n
        for j, ref in enumerate(outs[i * n : (i + 1) * n]):
            ref[...] = out[j * tall : (j + 1) * tall, :]


def finish(width, mask_ref, masked_ref, *refs):
    parts, g_ref, quad_ref = refs[:-2], refs[-2], refs[-1]
    rows = g_ref.shape[0]
    supers, blocks = mask_ref.shape
    tall = rows // blocks
    for b in range(blocks):
        for s in range(supers):
            cols = slice(s * width, (s + 1) * width)
            total = None
            for whole in parts:
                pieces = whole if isinstance(whole, tuple) else (whole,)
                depth = rows // len(pieces)
                ref, at = pieces[b * tall // depth], b * tall % depth
                term = ref[at : at + tall, cols]
                total = term if total is None else total + term
            g_ref[b * tall : (b + 1) * tall, cols] = total * -mask_ref[s, b].astype(F32)
    for s in range(supers if quad_ref is not None else 0):
        cols = slice(s * width, (s + 1) * width)
        mh, ml = split(masked_ref[:, cols])
        gh, gl = split(g_ref[:, cols])
        quad_ref[cols, :] = -(dot(mh, gh, ROWS) + (dot(mh, gl, ROWS) + dot(ml, gh, ROWS)))


def quad_only(width, mask_ref, masked_ref, own, near, *refs):
    *fars, g_ref, quad_ref = refs[:-2] + (refs[-1], refs[-2])
    finish(width, mask_ref, masked_ref, own, near, tuple(fars), g_ref, quad_ref)


def panel_only(width, mask_ref, own, near, *refs):
    finish(width, mask_ref, None, own, near, tuple(refs[:-1]), refs[-1], None)


def gather_any(side, masked, halves, swap):
    rows, cols = masked.shape
    turned = lax.ppermute(
        masked, GRID, [(r * side + c, c * side + r) for r in range(side) for c in range(side)]
    )
    turned, *halves = lax.optimization_barrier((turned, *halves))
    panels = {0: turned}
    bit = side // 2
    while bit:
        for j, x in list(panels.items()):
            panels[j ^ bit] = swap(x, "row", bit)
        bit //= 2
    shift = jnp.bitwise_xor(lax.axis_index("row"), lax.axis_index("col"))
    partials = call(
        functools.partial(products, side),
        [SMEM] + [VMEM] * (2 + side),
        [((rows, cols), F32)] * side,
        (shift.astype(jnp.int32).reshape(1), *halves, *[panels[j] for j in range(side)]),
        48,
        "products",
    )
    return [partials[0]] + [swap(partials[i], "col", i) for i in range(1, side)]


def route(rule):
    pairs = []
    for x in range(2):
        for t in range(2):
            for h in range(2):
                for l in range(2):
                    to = rule(x, t, h, l)
                    if to is not None:
                        (x2, t2), z2 = to
                        pairs.append((8 * x + 4 * t + 2 * h + l, 8 * x2 + 4 * t2 + z2))
    return pairs


def to_plane(x, t, h, l):
    return ((1 - h, t), 2 * h + l) if t == l else ((1 - h, 1 - t), 2 * h + t)


def cross_early(x, t, h, l):
    return to_plane(x, t, h, l) if x == h else ((1 - x, t), 2 * h + l)


def far_direct(x, t, h, l):
    return to_plane(x, t, h, l) if x == h else ((x, l), 2 * x + t)


def far_both(x, t, h, l):
    return ((x, l), 2 * (1 - x) + t) if x == h else ((x, l), 2 * x + t)


def move(x, rule, name):
    with jax.named_scope(name):
        return lax.ppermute(x, GRID, route(rule))


def after(x, *others):
    return lax.optimization_barrier((x, *others))[0]


def gather_four(masked, top, low, inverse_blocks, halved, swap):
    rows, cols = masked.shape
    row, col = lax.axis_index("row"), lax.axis_index("col")
    near_side = (row // 2) == (col // 2)
    same = ((row % 2) == (col % 2)).astype(jnp.int32).reshape(1)
    half, whole = ((rows // 2, cols), F32), ((rows, cols), F32)

    low_crossed = move(low, cross_early, "low_crossed")
    top_moved = move(top, far_direct, "top_moved")
    low_next = jnp.where(near_side, low_crossed, low)
    low_moved = move(low_next, far_both, "low_moved")
    halves = halved(after(inverse_blocks, low_next))
    low_flip = swap(after(low_crossed, *halves), "row", 2, "low_flip")
    top_flip = swap(top_moved, "row", 2, "top_flip")
    near = jnp.where(
        near_side,
        jnp.concatenate([top_flip, low_flip]),
        jnp.concatenate([top_moved, low_crossed]),
    )
    far = jnp.concatenate([jnp.where(near_side, top_moved, top_flip), low_moved])
    near_other = swap(near, "row", 1, "near_cores")

    far_other = swap(far, "row", 1, "far_cores")
    outs = call(
        pair, [SMEM] + [VMEM] * 4, [half] * 4, (same, *halves, far, far_other), 12, "far_pair"
    )
    two, three = outs[:2], outs[2:]
    own, near1 = call(
        pair, [SMEM] + [VMEM] * 4, [whole] * 2, (same, *halves, near, near_other), 12, "near_pair"
    )
    near1 = swap(near1, "col", 1, "near_partial")
    sums = [a + swap(b, "col", 1, "next") for a, b in zip(two, three)]
    return [own, near1, *[swap(x, "col", 2, "across") for x in sums]]


def on_device(side, inverse_blocks, lower_panel, struct_mask, diag_inverse):
    width = diag_inverse.shape[1]
    rows, cols = lower_panel.shape

    def swap(x, axis, bit, name="swap"):
        with jax.named_scope(name):
            return lax.ppermute(x, axis, [(i, i ^ bit) for i in range(side)])

    mask = struct_mask.T
    blocks = struct_mask.shape[0]
    four = side == 4 and blocks % 2 == 0

    def masked_rows(*spans, grant=4):
        return call(
            functools.partial(masking, spans),
            [SMEM, VMEM],
            [((rows * (last - first) // blocks, cols), F32) for first, last in spans],
            (mask, lower_panel),
            grant,
            "masking",
        )

    def halved(matrix):
        return call(
            splitting,
            [VMEM],
            [(matrix.shape, jnp.bfloat16)] * 2,
            (matrix,),
            8,
            "splitting",
            20_000_000_000,
        )

    if four:
        (low,) = masked_rows((blocks // 2, blocks), grant=60)
        masked, top = masked_rows((0, blocks), (0, blocks // 2))
        arrived = gather_four(masked, top, low, inverse_blocks, halved, swap)
    else:
        (masked,) = masked_rows((0, blocks))
        arrived = gather_any(side, masked, halved(inverse_blocks), swap)

    if four:
        (quad,) = call(
            functools.partial(quad_only, width),
            [SMEM] + [VMEM] * (1 + len(arrived)),
            [((cols, width), F32)],
            (mask, masked, *arrived),
            16,
            "quad",
            scratch=[pltpu.VMEM((rows, cols), F32)],
        )
        late = lax.optimization_barrier((quad, *arrived))[1:]
        (g_panel,) = call(
            functools.partial(panel_only, width),
            [SMEM] + [VMEM] * len(arrived),
            [((rows, cols), F32)],
            (mask, *late),
            16,
            "panel",
        )
    else:
        g_panel, quad = call(
            functools.partial(finish, width),
            [SMEM] + [VMEM] * (1 + len(arrived)),
            [((rows, cols), F32), ((cols, width), F32)],
            (mask, masked, *arrived),
            16,
            "finish",
        )
    if four:
        for part in [swap(quad, "row", bit, "tail") for bit in range(1, side)]:
            quad = quad + part
        return g_panel, diag_inverse + quad
    bit = 1
    while bit < side:
        quad = quad + swap(quad, "row", bit)
        bit *= 2
    return g_panel, diag_inverse + quad


def solution(mesh):
    side = mesh.shape["row"]
    assert side == mesh.shape["col"] and side & (side - 1) == 0
    placed = (
        P(("pole", "row"), "col"),
        P(("pole", "row"), "col"),
        P("row", "col"),
        P(("pole", "col"), None),
    )
    return jax.shard_map(
        functools.partial(on_device, side),
        mesh=mesh,
        in_specs=placed,
        out_specs=(P(("pole", "row"), "col"), P(("pole", "col"), None)),
        check_vma=False,
    )
```
